32 devices in a mesh: fsdp: 8 (over y, x, core), tp: 4 (over z).
Axes of the slice: x: 2, y: 2, z: 4, core: 2. Of those that a mesh axis runs over, the one named last changes fastest.
Arguments:
- hidden_in: bfloat16 [8192, 2048], P(('fsdp', 'tp')), may hold values from -6 to 6
- grad_out: bfloat16 [8192, 2048], P(('fsdp', 'tp')), may hold values from -6 to 6
- prefix_len: int32 [8], P('fsdp'), may hold values from 102 to 512
- positions: int32 [8192], P('fsdp'), may hold values from 0 to 4092, as said below
- g_attn: bfloat16 [2048], P('fsdp'), may hold values from 0.5 to 1.5
- w_query: bfloat16 [2048, 2048], P('fsdp', 'tp'), may hold values from -0.125 to 0.125
- w_key: bfloat16 [2048, 1024], P('fsdp', 'tp'), may hold values from -0.125 to 0.125
- w_value: bfloat16 [2048, 1024], P('fsdp', 'tp'), may hold values from -0.125 to 0.125
- w_out: bfloat16 [2048, 2048], P('tp', 'fsdp'), may hold values from -0.375 to 0.375
- q_gain: bfloat16 [128], P('fsdp'), may hold values from 0.796875 to 1.796875
- k_gain: bfloat16 [128], P('fsdp'), may hold values from 0.796875 to 1.796875
- g_ffn: bfloat16 [2048], P('fsdp'), may hold values from 0.5 to 1.5
- w_gate: bfloat16 [2048, 6144], P('fsdp', 'tp'), may hold values from -0.125 to 0.125
- w_up: bfloat16 [2048, 6144], P('fsdp', 'tp'), may hold values from -0.125 to 0.125
- w_down: bfloat16 [6144, 2048], P('tp', 'fsdp'), may hold values from -0.15625 to 0.15625
Outputs:
- out: bfloat16 [8192, 2048], P(('fsdp', 'tp'))
- d_x: float32 [8192, 2048], P(('fsdp', 'tp'))
- grad_g_attn: float32 [2048], P('fsdp')
- grad_w_query: float32 [2048, 2048], P('fsdp', 'tp')
- grad_w_key: float32 [2048, 1024], P('fsdp', 'tp')
- grad_w_value: float32 [2048, 1024], P('fsdp', 'tp')
- grad_w_out: float32 [2048, 2048], P('tp', 'fsdp')
- grad_q_gain: float32 [128], P('fsdp')
- grad_k_gain: float32 [128], P('fsdp')
- grad_g_ffn: float32 [2048], P('fsdp')
- grad_w_gate: float32 [2048, 6144], P('fsdp', 'tp')
- grad_w_up: float32 [2048, 6144], P('fsdp', 'tp')
- grad_w_down: float32 [6144, 2048], P('tp', 'fsdp')
The draws below stay inside these ranges and needn't reach their ends.
Inputs may be any that keep to these rules, and one draw needn't show every extreme that they name: The keys of sequence s at places below prefix_len[s] are seen by every query of that sequence. Within each sequence positions start at 0 and rise by 1 to 4 from token to token; in one sequence every rise is 4.
All inputs are finite; a program needn't handle non-finite values.
Results may differ from the reference program's by a relative error of at most 0.025.
Values may be sent and summed in bfloat16 or wider, within the bound.
A program may use at most 256 MiB of HBM per device.

```python
import math
import jax
import jax.numpy as jnp
from jax import lax

D = 2048
HEADS = 16
KV_HEADS = 8
HD = 128
FF = 6144
LEN = 1024
NSEQ = 8
TOKENS = 8192


def draw_positions(key, part):
    step_key = jax.random.fold_in(key, 11)
    pick_key = jax.random.fold_in(key, 12)
    steps_between = jax.random.randint(step_key, (NSEQ, LEN), 1, 5, dtype=jnp.int32)
    chosen = jax.random.randint(pick_key, (), 0, NSEQ, dtype=jnp.int32)
    rows = jnp.arange(NSEQ, dtype=jnp.int32)[:, None]
    steps_between = jnp.where(rows == chosen, jnp.int32(4), steps_between)
    rising = jnp.cumsum(steps_between, axis=1) - steps_between[:, 0:1]
    return rising.reshape(TOKENS).astype(jnp.int32)


def with_ends(values, own_key, least, high):
    index_at = [jax.random.randint(jax.random.fold_in(own_key, axis), (), 0, length) for axis, length in enumerate(values.shape)]
    longest = values.shape.index(max(values.shape))
    beside = index_at[:longest] + [(index_at[longest] + 1) % values.shape[longest]] + index_at[longest + 1:]
    return values.at[tuple(index_at)].set(least).at[tuple(beside)].set(high)


def levels(own_key, shape, pieces, least, top_value):
    factor_of = 1.0
    for dim, shards_of in pieces:
        heights = jax.random.uniform(jax.random.fold_in(jax.random.fold_in(own_key, 6), dim), (shards_of,), jnp.float32, least / len(pieces), top_value / len(pieces))
        factor_of = factor_of * jnp.repeat(jnp.exp(heights), shape[dim] // shards_of).reshape((-1,) + (1,) * (len(shape) - 1 - dim))
    return factor_of


def scatter_about(key, shape, deviation, limit, pieces=(), held_as=jnp.bfloat16):
    values = jax.random.normal(key, shape, jnp.float32) * deviation
    if len(pieces) > 0:
        values = levels(key, shape, pieces, -0.22, 0.18) * values
    return jnp.clip(values, min=-limit, max=limit).astype(held_as)


def setup_inputs(seed: int = 0) -> dict:
    splits = jax.random.split(jax.random.key(seed), 16)
    hidden_in = scatter_about(splits[0], (TOKENS, D), 1.0, 6.0, ((0, 32),))
    grad_out = scatter_about(splits[1], (TOKENS, D), 1.0, 6.0, ((0, 32),))
    prefix_len = with_ends(jax.random.randint(splits[2], (NSEQ,), LEN // 10, LEN // 2 + 1), jax.random.fold_in(splits[2], 1), LEN // 10, (LEN // 2 + 1) - 1).astype(jnp.int32)
    positions = draw_positions(jax.random.fold_in(splits[15], 71), 0)
    g_attn = jnp.clip(0.5 + 1.0 * jax.random.uniform(splits[4], (D,), jnp.float32) ** levels(splits[4], (D,), ((0, 8),), -0.2, 0.2), 0.5, 1.5).astype(jnp.bfloat16)
    w_query = scatter_about(splits[5], (D, HEADS * HD), D ** -0.5, 0.125, ((0, 8), (1, 4)))
    w_key = scatter_about(splits[6], (D, KV_HEADS * HD), D ** -0.5, 0.125, ((0, 8), (1, 4)))
    w_value = scatter_about(splits[7], (D, KV_HEADS * HD), D ** -0.5, 0.125, ((0, 8), (1, 4)))
    w_out = scatter_about(splits[8], (HEADS * HD, D), (HEADS * HD // 8) ** -0.5, 0.375, ((0, 4), (1, 8)))
    q_gain = jnp.clip(0.796875 + 1.0 * jax.random.uniform(splits[9], (HD,), jnp.float32) ** levels(splits[9], (HD,), ((0, 8),), -0.2, 0.2), 0.796875, 1.796875).astype(jnp.bfloat16)
    k_gain = jnp.clip(0.796875 + 1.0 * jax.random.uniform(splits[10], (HD,), jnp.float32) ** levels(splits[10], (HD,), ((0, 8),), -0.2, 0.2), 0.796875, 1.796875).astype(jnp.bfloat16)
    g_ffn = jnp.clip(0.5 + 1.0 * jax.random.uniform(splits[11], (D,), jnp.float32) ** levels(splits[11], (D,), ((0, 8),), -0.2, 0.2), 0.5, 1.5).astype(jnp.bfloat16)
    w_gate = scatter_about(splits[12], (D, FF), D ** -0.5, 0.125, ((0, 8), (1, 4)))
    w_up = scatter_about(splits[13], (D, FF), D ** -0.5, 0.125, ((0, 8), (1, 4)))
    w_down = scatter_about(splits[14], (FF, D), (FF // 4) ** -0.5, 0.15625, ((0, 4), (1, 8)))
    return dict(hidden_in=hidden_in, grad_out=grad_out, prefix_len=prefix_len, positions=positions, g_attn=g_attn, w_query=w_query, w_key=w_key, w_value=w_value, w_out=w_out, q_gain=q_gain, k_gain=k_gain, g_ffn=g_ffn, w_gate=w_gate, w_up=w_up, w_down=w_down)


EPS = 1e-06
ROPE_BASE = 1000000.0

@jax.custom_vjp
def low(v):
    return lax.optimization_barrier(v.astype(jnp.bfloat16)).astype(jnp.float32)

@jax.custom_vjp
def low_back(v):
    return v

def low_keep(v):
    return (low(v), None)

def low_pass(kept, grad):
    return (grad,)

def back_keep(v):
    return (v, None)

def back_low(kept, grad):
    return (low(grad),)
low.defvjp(low_keep, low_pass)
low_back.defvjp(back_keep, back_low)

def rms_scale(value):
    return lax.rsqrt(lax.optimization_barrier(jnp.mean(value * value, axis=-1, keepdims=True)) + EPS)

def matmul(left, right):
    return jnp.dot(left, right, precision=lax.Precision.HIGHEST, preferred_element_type=jnp.float32)

def rope_tables(places):
    half = HD // 2
    ladder = jnp.arange(half, dtype=jnp.float32) * (2.0 / HD)
    frequency = jnp.exp(-ladder * math.log(ROPE_BASE))
    angle = places.astype(jnp.float32)[:, None] * frequency[None, :]
    return (jnp.cos(angle), jnp.sin(angle))

def rotate(value, cosine, sine):
    half = value.shape[-1] // 2
    first = value[..., :half]
    second = value[..., half:]
    return jnp.concatenate([first * cosine - second * sine, second * cosine + first * sine], axis=-1)

def attend_one(query, keys, values, prefix):
    group = HEADS // KV_HEADS
    query = query.reshape(LEN, KV_HEADS, group, HD)
    scores = jnp.einsum('qkgd,pkd->kgqp', query, keys, precision=lax.Precision.HIGHEST)
    scores = low_back(scores) * (1.0 / math.sqrt(HD))
    places = jnp.arange(LEN, dtype=jnp.int32)
    visible = (places[None, :] <= places[:, None]) | (places[None, :] < prefix)
    scores = jnp.where(visible, scores, -1e+30)
    shares = jax.nn.softmax(scores, axis=-1)
    mixed = jnp.einsum('kgqp,pkd->qkgd', low(shares), values, precision=lax.Precision.HIGHEST)
    return mixed.reshape(LEN, HEADS * HD)

def attend_item(item):
    return attend_one(item[0], item[1], item[2], item[3])

def layer(params, tokens, prefix, places):
    g_attn, w_query, w_key, w_value, w_out, q_gain, k_gain, g_ffn, w_gate, w_up, w_down = params
    count = prefix.shape[0]
    total = tokens.shape[0]
    normed = low(tokens * rms_scale(tokens) * g_attn)
    query = low_back(matmul(normed, w_query)).reshape(total, HEADS, HD)
    keys = low_back(matmul(normed, w_key)).reshape(total, KV_HEADS, HD)
    values = low(low_back(matmul(normed, w_value))).reshape(total, KV_HEADS, HD)
    cosine, sine = rope_tables(places)
    cosine = cosine[:, None, :]
    sine = sine[:, None, :]
    query = low(rotate(query * rms_scale(query) * q_gain, cosine, sine))
    keys = low(rotate(keys * rms_scale(keys) * k_gain, cosine, sine))
    mixed = lax.map(jax.checkpoint(attend_item), (query.reshape(count, LEN, HEADS, HD), keys.reshape(count, LEN, KV_HEADS, HD), values.reshape(count, LEN, KV_HEADS, HD), prefix))
    mixed = low(low_back(mixed.reshape(total, HEADS * HD)))
    middle = tokens + low_back(matmul(mixed, w_out))
    branch = low(middle * rms_scale(middle) * g_ffn)
    gate = low_back(matmul(branch, w_gate))
    upward = low_back(matmul(branch, w_up))
    product = low(jax.nn.silu(gate) * upward)
    return middle + low_back(matmul(product, w_down))

def reference(hidden_in, grad_out, prefix_len, positions, g_attn, w_query, w_key, w_value, w_out, q_gain, k_gain, g_ffn, w_gate, w_up, w_down):
    batch = math.gcd(NSEQ, max(1, 4096 // LEN))
    blocks = NSEQ // batch
    params = tuple((weight.astype(jnp.float32) for weight in (g_attn, w_query, w_key, w_value, w_out, q_gain, k_gain, g_ffn, w_gate, w_up, w_down)))

    def run(params, tokens):

        def step(carry, item):
            block_tokens, block_prefix, block_places = item
            return (carry, jax.checkpoint(layer)(params, block_tokens, block_prefix, block_places))
        carry, result = lax.scan(step, None, (tokens.reshape(blocks, batch * LEN, D), prefix_len.reshape(blocks, batch), positions.reshape(blocks, batch * LEN)))
        return result.reshape(TOKENS, D)
    outputs, pull = jax.vjp(run, params, hidden_in.astype(jnp.float32))
    grads, grad_in = pull(grad_out.astype(jnp.float32))
    return (outputs.astype(jnp.bfloat16), grad_in, grads[0], grads[1], grads[2], grads[3], grads[4], grads[5], grads[6], grads[7], grads[8], grads[9], grads[10])
```

```python
import functools
import math

import jax
import jax.numpy as jnp
from jax import lax
from jax.experimental import pallas as pl
from jax.experimental.pallas import tpu as pltpu
from jax.sharding import PartitionSpec as P

MESH = pl.DeviceIdType.MESH

HD = 128


EPS = 1e-06
ROPE_BASE = 1000000.0


def rms_scale(value):
    return lax.rsqrt(jnp.mean(value * value, axis=-1, keepdims=True) + EPS)


def norm_gain(value, gain):
    return value * rms_scale(value) * gain


def rope_tables(places):
    half = HD // 2
    ladder = jnp.arange(half, dtype=jnp.float32) * (2.0 / HD)
    frequency = jnp.exp(-ladder * math.log(ROPE_BASE))
    angle = places.astype(jnp.float32)[:, None] * frequency[None, :]
    return (jnp.cos(angle)[:, None, :], jnp.sin(angle)[:, None, :])


def rotate(value, cosine, sine):
    half = value.shape[-1] // 2
    first = value[..., :half]
    second = value[..., half:]
    return jnp.concatenate(
        [first * cosine - second * sine, second * cosine + first * sine], axis=-1
    )


def head_prep(raw, gain, cosine, sine):
    return rotate(norm_gain(raw, gain), cosine, sine)


def visibility(length, prefix):
    places = jnp.arange(length, dtype=jnp.int32)
    return (places[None, :] <= places[:, None]) | (places[None, :] < prefix)


def masked_scores(query, keys, prefix):
    scale = 1.0 / math.sqrt(HD)
    scores = jnp.einsum("qkgd,pkd->kgqp", query, keys, preferred_element_type=jnp.float32) * scale
    return jnp.where(visibility(query.shape[0], prefix), scores, -1e30)


def attend_forward(item):
    query, keys, values, prefix = item
    scores = masked_scores(query, keys, prefix)
    peak = jnp.max(scores, axis=-1, keepdims=True)
    raised = jnp.exp(scores - peak)
    total = jnp.sum(raised, axis=-1, keepdims=True)
    shares = raised / total
    mixed = jnp.einsum(
        "kgqp,pkd->qkgd", shares.astype(jnp.bfloat16), values, preferred_element_type=jnp.float32
    )
    return (mixed, (peak + jnp.log(total))[..., 0])


def attend_backward(item):
    query, keys, values, grad_mixed, log_total, prefix = item
    scale = 1.0 / math.sqrt(HD)
    scores = masked_scores(query, keys, prefix)
    shares = jnp.exp(scores - log_total[..., None])
    grad_shares = jnp.einsum(
        "qkgd,pkd->kgqp", grad_mixed, values, preferred_element_type=jnp.float32
    )
    grad_scores = shares * (grad_shares - jnp.sum(grad_shares * shares, axis=-1, keepdims=True))
    grad_low = (grad_scores * scale).astype(jnp.bfloat16)
    grad_query = jnp.einsum("kgqp,pkd->qkgd", grad_low, keys, preferred_element_type=jnp.float32)
    grad_keys = jnp.einsum("kgqp,qkgd->pkd", grad_low, query, preferred_element_type=jnp.float32)
    grad_values = jnp.einsum(
        "kgqp,qkgd->pkd",
        shares.astype(jnp.bfloat16),
        grad_mixed,
        preferred_element_type=jnp.float32,
    )
    return (grad_query, grad_keys, grad_values)


def greet(me, n, axis):
    barrier = pltpu.get_barrier_semaphore()
    for d in (1, -1):
        @pl.when((me + d >= 0) & (me + d < n))
        def _():
            pl.semaphore_signal(barrier, inc=1, device_id={axis: me + d}, device_id_type=MESH)
    edge = (me == 0) | (me == n - 1)

    @pl.when(edge)
    def _():
        pl.semaphore_wait(barrier, 1)

    @pl.when(~edge)
    def _():
        pl.semaphore_wait(barrier, 2)

def inside(v, n):
    return (v >= 0) & (v < n)

def ag_kernel(n, S, axis, x_ref, o_ref, send_sem, recv_sem):
    me = lax.axis_index(axis)
    R = x_ref.shape[0]; sub = R // S
    greet(me, n, axis)
    def rows(j, s):
        return pl.ds(pl.multiple_of(j * R + s * sub, sub), sub)
    def item(di, d, k, s, sender):
        j = sender - d * k
        src = x_ref.at[pl.ds(s * sub, sub)] if k == 0 else o_ref.at[rows(j, s)]
        return pltpu.make_async_remote_copy(src_ref=src, dst_ref=o_ref.at[rows(j, s)], send_sem=send_sem.at[di, k, s], recv_sem=recv_sem.at[di, k, s], device_id={axis: sender + d}, device_id_type=MESH)
    for k in range(n):
        for s in range(S):
            for di, d in enumerate((1, -1)):
                if k > 0:
                    @pl.when(inside(me - d * k, n))
                    def _():
                        item(di, d, k - 1, s, me - d).wait_recv()
                if k < n - 1:
                    @pl.when(inside(me - d * k, n) & inside(me + d, n))
                    def _():
                        item(di, d, k, s, me).start()
        if k == 0:
            o_ref[pl.ds(pl.multiple_of(me * R, R), R), :] = x_ref[...]
    for k in range(n - 1):
        for s in range(S):
            for di, d in enumerate((1, -1)):
                @pl.when(inside(me - d * k, n) & inside(me + d, n))
                def _():
                    item(di, d, k, s, me).wait_send()

def ag(x, n, S=2, axis="tp", cid=1):
    R, D = x.shape
    return pl.pallas_call(functools.partial(ag_kernel, n, S, axis),
        out_shape=jax.ShapeDtypeStruct((n * R, D), x.dtype),
        in_specs=[pl.BlockSpec(memory_space=pltpu.VMEM)],
        out_specs=pl.BlockSpec(memory_space=pltpu.VMEM),
        scratch_shapes=[pltpu.SemaphoreType.DMA((2, n - 1, S)), pltpu.SemaphoreType.DMA((2, n - 1, S))],
        compiler_params=pltpu.CompilerParams(collective_id=cid, has_side_effects=True, vmem_limit_bytes=32 << 20), name="ag")(x)

def rs_kernel(n, S, axis, p_ref, o_ref, rb, send_sem, recv_sem):
    me = lax.axis_index(axis)
    R = o_ref.shape[0]; sub = R // S
    greet(me, n, axis)
    def rows(j, s):
        return pl.ds(pl.multiple_of(j * R + s * sub, sub), sub)
    def at(s):
        return pl.ds(s * sub, sub)
    def owner(d, q):
        return n - 1 - q if d > 0 else q
    def item(di, d, q, s, sender, first):
        src = p_ref.at[rows(owner(d, q), s)] if first else rb.at[di, q, at(s)]
        return pltpu.make_async_remote_copy(src_ref=src, dst_ref=rb.at[di, q, at(s)], send_sem=send_sem.at[di, q, s], recv_sem=recv_sem.at[di, q, s], device_id={axis: sender + d}, device_id_type=MESH)
    ways = ((0, 1, me), (1, -1, n - 1 - me))
    for q in range(n - 1):
        for s in range(S):
            for di, d, dist in ways:
                @pl.when(dist == 0)
                def _():
                    item(di, d, q, s, me, True).start()
    for t in range(1, n - 1):
        for s in range(S):
            for di, d, dist in ways:
                @pl.when((dist > 0) & (t >= dist))
                def _():
                    q = t - dist
                    item(di, d, q, s, me - d, False).wait_recv()
                    rb[di, q, at(s), :] = (rb[di, q, at(s), :].astype(jnp.float32) + p_ref[rows(owner(d, q), s), :].astype(jnp.float32)).astype(rb.dtype)
                    item(di, d, q, s, me, False).start()
    for s in range(S):
        for di, d, dist in ways:
            @pl.when(dist > 0)
            def _():
                item(di, d, n - 1 - dist, s, me - d, False).wait_recv()
        @pl.when(me == 0)
        def _():
            o_ref[at(s), :] = p_ref[rows(0, s), :].astype(jnp.float32) + rb[1, 0, at(s), :].astype(jnp.float32)
        @pl.when(me == n - 1)
        def _():
            o_ref[at(s), :] = p_ref[rows(n - 1, s), :].astype(jnp.float32) + rb[0, 0, at(s), :].astype(jnp.float32)
        @pl.when((me > 0) & (me < n - 1))
        def _():
            o_ref[at(s), :] = p_ref[rows(me, s), :].astype(jnp.float32) + rb[0, n - 1 - me, at(s), :].astype(jnp.float32) + rb[1, me, at(s), :].astype(jnp.float32)
    for t in range(0, n - 1):
        for s in range(S):
            for di, d, dist in ways:
                @pl.when(t >= dist)
                def _():
                    item(di, d, t - dist, s, me, False).wait_send()

def rs(p, n, S=2, axis="tp", cid=2):
    NR, D = p.shape; R = NR // n
    return pl.pallas_call(functools.partial(rs_kernel, n, S, axis),
        out_shape=jax.ShapeDtypeStruct((R, D), jnp.float32),
        in_specs=[pl.BlockSpec(memory_space=pltpu.VMEM)],
        out_specs=pl.BlockSpec(memory_space=pltpu.VMEM),
        scratch_shapes=[pltpu.VMEM((2, n - 1, R, D), p.dtype), pltpu.SemaphoreType.DMA((2, n - 1, S)), pltpu.SemaphoreType.DMA((2, n - 1, S))],
        compiler_params=pltpu.CompilerParams(collective_id=cid, has_side_effects=True, vmem_limit_bytes=32 << 20), name="rs")(p)

def per_device(
    hidden_in,
    grad_out,
    prefix_len,
    positions,
    g_attn,
    w_query,
    w_key,
    w_value,
    w_out,
    q_gain,
    k_gain,
    g_ffn,
    w_gate,
    w_up,
    w_down,
):
    parts = lax.axis_size("tp")
    groups = lax.axis_size("fsdp")
    own_rows, width = hidden_in.shape
    group_rows = own_rows * parts
    count = prefix_len.shape[0]
    length = group_rows // count
    qc, kc, fc = w_query.shape[1], w_key.shape[1], w_gate.shape[1]
    slot = g_attn.shape[0]
    head_slot = q_gain.shape[0]
    packed = jnp.concatenate([g_attn, g_ffn, q_gain, k_gain])[None]
    gains = lax.all_gather(packed, "fsdp", axis=0, tiled=True).astype(jnp.float32)
    first_gain = gains[:, :slot].reshape(-1)
    second_gain = gains[:, slot : 2 * slot].reshape(-1)
    query_gain = gains[:, 2 * slot : 2 * slot + head_slot].reshape(-1)
    key_gain = gains[:, 2 * slot + head_slot :].reshape(-1)
    attn_set = lax.all_gather(
        jnp.concatenate([w_query, w_key, w_value, w_out.T], axis=1), "fsdp", axis=0, tiled=True
    )
    full_qkv = attn_set[:, : qc + 2 * kc]
    full_out = attn_set[:, qc + 2 * kc :]
    ffn_set = lax.all_gather(
        jnp.concatenate([w_gate, w_up, w_down.T], axis=1), "fsdp", axis=0, tiled=True
    )
    full_gate, full_up, full_down = ffn_set[:, :fc], ffn_set[:, fc : 2 * fc], ffn_set[:, 2 * fc :]

    tokens_all = ag(hidden_in, parts, cid=1)
    tokens_float = tokens_all.astype(jnp.float32)
    own_float = hidden_in.astype(jnp.float32)
    normed = norm_gain(tokens_float, first_gain).astype(jnp.bfloat16)
    raw = jnp.dot(normed, full_qkv, preferred_element_type=jnp.float32)
    query_raw = raw[:, :qc].reshape(group_rows, -1, HD)
    keys_raw = raw[:, qc : qc + kc].reshape(group_rows, -1, HD)
    values_low = raw[:, qc + kc :].astype(jnp.bfloat16).reshape(group_rows, -1, HD)
    kv_local = keys_raw.shape[1]
    grouping = query_raw.shape[1] // kv_local
    cosine, sine = rope_tables(positions)
    query_low = head_prep(query_raw, query_gain, cosine, sine).astype(jnp.bfloat16)
    keys_low = head_prep(keys_raw, key_gain, cosine, sine).astype(jnp.bfloat16)
    query_seq = query_low.reshape(count, length, kv_local, grouping, HD)
    keys_seq = keys_low.reshape(count, length, kv_local, HD)
    values_seq = values_low.reshape(count, length, kv_local, HD)
    mixed, log_total = lax.map(attend_forward, (query_seq, keys_seq, values_seq, prefix_len))
    mixed_low = mixed.reshape(group_rows, -1).astype(jnp.bfloat16)
    attn_part = jnp.einsum("th,dh->td", mixed_low, full_out, preferred_element_type=jnp.float32)
    middle = own_float + rs(attn_part.astype(jnp.bfloat16), parts, cid=2)
    branch = ag(norm_gain(middle, second_gain).astype(jnp.bfloat16), parts, cid=3)
    gate = jnp.dot(branch, full_gate, preferred_element_type=jnp.float32)
    upward = jnp.dot(branch, full_up, preferred_element_type=jnp.float32)
    sigmoid_gate = jax.nn.sigmoid(gate)
    silu_gate = gate * sigmoid_gate
    product = (silu_gate * upward).astype(jnp.bfloat16)
    ffn_part = jnp.einsum("tf,df->td", product, full_down, preferred_element_type=jnp.float32)
    result = middle + lax.psum_scatter(
        ffn_part.astype(jnp.bfloat16), "tp", scatter_dimension=0, tiled=True
    ).astype(jnp.float32)
    out = result.astype(jnp.bfloat16)
    grad_all = lax.all_gather(grad_out, "tp", axis=0, tiled=True)
    grad_product = jnp.dot(grad_all, full_down, preferred_element_type=jnp.float32)
    grad_w_down = jnp.einsum("td,tf->df", grad_all, product, preferred_element_type=jnp.float32)
    grad_gate = (
        grad_product * upward * (sigmoid_gate * (1.0 + gate * (1.0 - sigmoid_gate)))
    ).astype(jnp.bfloat16)
    grad_up = (grad_product * silu_gate).astype(jnp.bfloat16)
    grad_w_gate = jnp.einsum("td,tf->df", branch, grad_gate, preferred_element_type=jnp.float32)
    grad_w_up = jnp.einsum("td,tf->df", branch, grad_up, preferred_element_type=jnp.float32)
    grad_branch = jnp.einsum("tf,df->td", grad_gate, full_gate, preferred_element_type=jnp.float32)
    grad_branch = grad_branch + jnp.einsum(
        "tf,df->td", grad_up, full_up, preferred_element_type=jnp.float32
    )
    grad_branch_own = rs(grad_branch.astype(jnp.bfloat16), parts, cid=4)
    unused_second, pull_second = jax.vjp(norm_gain, middle, second_gain)
    grad_mid_norm, grad_second = pull_second(grad_branch_own)
    grad_middle = grad_out.astype(jnp.float32) + grad_mid_norm
    grad_mid_all = ag(grad_middle.astype(jnp.bfloat16), parts, cid=5)

    def spread(value):
        return lax.psum_scatter(
            value.astype(jnp.bfloat16), "fsdp", scatter_dimension=0, tiled=True
        ).astype(jnp.float32)

    down_own = spread(grad_w_down)
    gate_own = spread(grad_w_gate)
    up_own = spread(grad_w_up)
    grad_mixed = jnp.dot(grad_mid_all, full_out, preferred_element_type=jnp.float32).astype(
        jnp.bfloat16
    )
    grad_w_out = jnp.einsum(
        "td,th->dh", grad_mid_all, mixed_low, preferred_element_type=jnp.float32
    )
    grad_mixed_seq = grad_mixed.reshape(count, length, kv_local, grouping, HD)
    grads_query, grads_keys, grads_values = lax.map(
        attend_backward, (query_seq, keys_seq, values_seq, grad_mixed_seq, log_total, prefix_len)
    )
    unused_query, pull_query = jax.vjp(
        functools.partial(head_prep, cosine=cosine, sine=sine), query_raw, query_gain
    )
    grad_query_raw, grad_q_gain = pull_query(grads_query.reshape(group_rows, -1, HD))
    unused_keys, pull_keys = jax.vjp(
        functools.partial(head_prep, cosine=cosine, sine=sine), keys_raw, key_gain
    )
    grad_keys_raw, grad_k_gain = pull_keys(grads_keys.reshape(group_rows, -1, HD))
    grad_qkv = jnp.concatenate(
        [
            grad_query_raw.reshape(group_rows, -1),
            grad_keys_raw.reshape(group_rows, -1),
            grads_values.reshape(group_rows, -1),
        ],
        axis=1,
    ).astype(jnp.bfloat16)
    grad_w_qkv = jnp.einsum("td,th->dh", normed, grad_qkv, preferred_element_type=jnp.float32)
    grad_normed = jnp.einsum("th,dh->td", grad_qkv, full_qkv, preferred_element_type=jnp.float32)
    out_own = spread(grad_w_out)
    qkv_own = spread(grad_w_qkv)
    grad_normed_own = rs(grad_normed.astype(jnp.bfloat16), parts, cid=6)
    unused_first, pull_first = jax.vjp(norm_gain, own_float, first_gain)
    grad_tokens, grad_first = pull_first(grad_normed_own)
    grad_in = grad_middle + grad_tokens
    sums = lax.psum(
        jnp.concatenate([grad_first, grad_second, grad_q_gain, grad_k_gain]), ("fsdp", "tp")
    )
    place = lax.axis_index("fsdp")
    wide = groups * slot
    narrow = groups * head_slot
    gain_first = lax.dynamic_slice_in_dim(sums, place * slot, slot)
    gain_second = lax.dynamic_slice_in_dim(sums, wide + place * slot, slot)
    gain_query = lax.dynamic_slice_in_dim(sums, 2 * wide + place * head_slot, head_slot)
    gain_key = lax.dynamic_slice_in_dim(sums, 2 * wide + narrow + place * head_slot, head_slot)
    return (
        out,
        grad_in,
        gain_first,
        qkv_own[:, :qc],
        qkv_own[:, qc : qc + kc],
        qkv_own[:, qc + kc :],
        out_own.T,
        gain_query,
        gain_key,
        gain_second,
        gate_own,
        up_own,
        down_own.T,
    )


def solution(mesh):
    in_specs = (
        P(("fsdp", "tp"), None),
        P(("fsdp", "tp"), None),
        P("fsdp"),
        P("fsdp"),
        P("fsdp"),
        P("fsdp", "tp"),
        P("fsdp", "tp"),
        P("fsdp", "tp"),
        P("tp", "fsdp"),
        P("fsdp"),
        P("fsdp"),
        P("fsdp"),
        P("fsdp", "tp"),
        P("fsdp", "tp"),
        P("tp", "fsdp"),
    )
    out_specs = (
        P(("fsdp", "tp"), None),
        P(("fsdp", "tp"), None),
        P("fsdp"),
        P("fsdp", "tp"),
        P("fsdp", "tp"),
        P("fsdp", "tp"),
        P("tp", "fsdp"),
        P("fsdp"),
        P("fsdp"),
        P("fsdp"),
        P("fsdp", "tp"),
        P("fsdp", "tp"),
        P("tp", "fsdp"),
    )
    return jax.shard_map(
        per_device, mesh=mesh, in_specs=in_specs, out_specs=out_specs, check_vma=False
    )
```

```python
import functools
import math

import jax
import jax.numpy as jnp
from jax import lax
from jax.experimental import pallas as pl
from jax.experimental.pallas import tpu as pltpu
from jax.sharding import PartitionSpec as P

MESH = pl.DeviceIdType.MESH
VMEM_LIMIT = 67043328

HD = 128


EPS = 1e-06
ROPE_BASE = 1000000.0


def rms_scale(value):
    return lax.rsqrt(jnp.mean(value * value, axis=-1, keepdims=True) + EPS)


def norm_gain(value, gain):
    return value * rms_scale(value) * gain


def rope_tables(places):
    half = HD // 2
    ladder = jnp.arange(half, dtype=jnp.float32) * (2.0 / HD)
    frequency = jnp.exp(-ladder * math.log(ROPE_BASE))
    angle = places.astype(jnp.float32)[:, None] * frequency[None, :]
    return (jnp.cos(angle)[:, None, :], jnp.sin(angle)[:, None, :])


def rotate(value, cosine, sine):
    half = value.shape[-1] // 2
    first = value[..., :half]
    second = value[..., half:]
    return jnp.concatenate(
        [first * cosine - second * sine, second * cosine + first * sine], axis=-1
    )


def head_prep(raw, gain, cosine, sine):
    return rotate(norm_gain(raw, gain), cosine, sine)


def visibility(length, prefix):
    places = jnp.arange(length, dtype=jnp.int32)
    return (places[None, :] <= places[:, None]) | (places[None, :] < prefix)


def masked_scores(query, keys, prefix):
    scale = 1.0 / math.sqrt(HD)
    scores = jnp.einsum("qkgd,pkd->kgqp", query, keys, preferred_element_type=jnp.float32) * scale
    return jnp.where(visibility(query.shape[0], prefix), scores, -1e30)


def attend_forward(item):
    query, keys, values, prefix = item
    scores = masked_scores(query, keys, prefix)
    peak = jnp.max(scores, axis=-1, keepdims=True)
    raised = jnp.exp(scores - peak)
    total = jnp.sum(raised, axis=-1, keepdims=True)
    shares = raised / total
    mixed = jnp.einsum(
        "kgqp,pkd->qkgd", shares.astype(jnp.bfloat16), values, preferred_element_type=jnp.float32
    )
    return (mixed, (peak + jnp.log(total))[..., 0])


def attend_backward(item):
    query, keys, values, grad_mixed, log_total, prefix = item
    scale = 1.0 / math.sqrt(HD)
    scores = masked_scores(query, keys, prefix)
    shares = jnp.exp(scores - log_total[..., None])
    grad_shares = jnp.einsum(
        "qkgd,pkd->kgqp", grad_mixed, values, preferred_element_type=jnp.float32
    )
    grad_scores = shares * (grad_shares - jnp.sum(grad_shares * shares, axis=-1, keepdims=True))
    grad_low = (grad_scores * scale).astype(jnp.bfloat16)
    grad_query = jnp.einsum("kgqp,pkd->qkgd", grad_low, keys, preferred_element_type=jnp.float32)
    grad_keys = jnp.einsum("kgqp,qkgd->pkd", grad_low, query, preferred_element_type=jnp.float32)
    grad_values = jnp.einsum(
        "kgqp,qkgd->pkd",
        shares.astype(jnp.bfloat16),
        grad_mixed,
        preferred_element_type=jnp.float32,
    )
    return (grad_query, grad_keys, grad_values)


def greet(me, n, axis):
    barrier = pltpu.get_barrier_semaphore()
    for d in (1, -1):
        @pl.when((me + d >= 0) & (me + d < n))
        def _():
            pl.semaphore_signal(barrier, inc=1, device_id={axis: me + d}, device_id_type=MESH)
    edge = (me == 0) | (me == n - 1)

    @pl.when(edge)
    def _():
        pl.semaphore_wait(barrier, 1)

    @pl.when(~edge)
    def _():
        pl.semaphore_wait(barrier, 2)

def inside(v, n):
    return (v >= 0) & (v < n)

def ag_kernel(n, S, axis, x_ref, o_ref, send_sem, recv_sem):
    me = lax.axis_index(axis)
    R = x_ref.shape[0]; sub = R // S
    greet(me, n, axis)
    def rows(j, s):
        return pl.ds(pl.multiple_of(j * R + s * sub, sub), sub)
    def item(di, d, k, s, sender):
        j = sender - d * k
        src = x_ref.at[pl.ds(s * sub, sub)] if k == 0 else o_ref.at[rows(j, s)]
        return pltpu.make_async_remote_copy(src_ref=src, dst_ref=o_ref.at[rows(j, s)], send_sem=send_sem.at[di, k, s], recv_sem=recv_sem.at[di, k, s], device_id={axis: sender + d}, device_id_type=MESH)
    for k in range(n):
        for s in range(S):
            for di, d in enumerate((1, -1)):
                if k > 0:
                    @pl.when(inside(me - d * k, n))
                    def _():
                        item(di, d, k - 1, s, me - d).wait_recv()
                if k < n - 1:
                    @pl.when(inside(me - d * k, n) & inside(me + d, n))
                    def _():
                        item(di, d, k, s, me).start()
        if k == 0:
            o_ref[pl.ds(pl.multiple_of(me * R, R), R), :] = x_ref[...]
    for k in range(n - 1):
        for s in range(S):
            for di, d in enumerate((1, -1)):
                @pl.when(inside(me - d * k, n) & inside(me + d, n))
                def _():
                    item(di, d, k, s, me).wait_send()

def ag(x, n, S=2, axis="tp", cid=1):
    R, D = x.shape
    return pl.pallas_call(functools.partial(ag_kernel, n, S, axis),
        out_shape=jax.ShapeDtypeStruct((n * R, D), x.dtype),
        in_specs=[pl.BlockSpec(memory_space=pltpu.VMEM)],
        out_specs=pl.BlockSpec(memory_space=pltpu.VMEM),
        scratch_shapes=[pltpu.SemaphoreType.DMA((2, n - 1, S)), pltpu.SemaphoreType.DMA((2, n - 1, S))],
        compiler_params=pltpu.CompilerParams(collective_id=cid, has_side_effects=True, vmem_limit_bytes=32 << 20), name="ag")(x)

def rs_kernel(n, S, axis, p_ref, o_ref, rb, send_sem, recv_sem):
    me = lax.axis_index(axis)
    R = o_ref.shape[0]; sub = R // S
    greet(me, n, axis)
    def rows(j, s):
        return pl.ds(pl.multiple_of(j * R + s * sub, sub), sub)
    def at(s):
        return pl.ds(s * sub, sub)
    def owner(d, q):
        return n - 1 - q if d > 0 else q
    def item(di, d, q, s, sender, first):
        src = p_ref.at[rows(owner(d, q), s)] if first else rb.at[di, q, at(s)]
        return pltpu.make_async_remote_copy(src_ref=src, dst_ref=rb.at[di, q, at(s)], send_sem=send_sem.at[di, q, s], recv_sem=recv_sem.at[di, q, s], device_id={axis: sender + d}, device_id_type=MESH)
    ways = ((0, 1, me), (1, -1, n - 1 - me))
    for q in range(n - 1):
        for s in range(S):
            for di, d, dist in ways:
                @pl.when(dist == 0)
                def _():
                    item(di, d, q, s, me, True).start()
    for t in range(1, n - 1):
        for s in range(S):
            for di, d, dist in ways:
                @pl.when((dist > 0) & (t >= dist))
                def _():
                    q = t - dist
                    item(di, d, q, s, me - d, False).wait_recv()
                    rb[di, q, at(s), :] = (rb[di, q, at(s), :].astype(jnp.float32) + p_ref[rows(owner(d, q), s), :].astype(jnp.float32)).astype(rb.dtype)
                    item(di, d, q, s, me, False).start()
    for s in range(S):
        for di, d, dist in ways:
            @pl.when(dist > 0)
            def _():
                item(di, d, n - 1 - dist, s, me - d, False).wait_recv()
        @pl.when(me == 0)
        def _():
            o_ref[at(s), :] = p_ref[rows(0, s), :].astype(jnp.float32) + rb[1, 0, at(s), :].astype(jnp.float32)
        @pl.when(me == n - 1)
        def _():
            o_ref[at(s), :] = p_ref[rows(n - 1, s), :].astype(jnp.float32) + rb[0, 0, at(s), :].astype(jnp.float32)
        @pl.when((me > 0) & (me < n - 1))
        def _():
            o_ref[at(s), :] = p_ref[rows(me, s), :].astype(jnp.float32) + rb[0, n - 1 - me, at(s), :].astype(jnp.float32) + rb[1, me, at(s), :].astype(jnp.float32)
    for t in range(0, n - 1):
        for s in range(S):
            for di, d, dist in ways:
                @pl.when(t >= dist)
                def _():
                    item(di, d, t - dist, s, me, False).wait_send()

def rs(p, n, S=2, axis="tp", cid=2):
    NR, D = p.shape; R = NR // n
    return pl.pallas_call(functools.partial(rs_kernel, n, S, axis),
        out_shape=jax.ShapeDtypeStruct((R, D), jnp.float32),
        in_specs=[pl.BlockSpec(memory_space=pltpu.VMEM)],
        out_specs=pl.BlockSpec(memory_space=pltpu.VMEM),
        scratch_shapes=[pltpu.VMEM((2, n - 1, R, D), p.dtype), pltpu.SemaphoreType.DMA((2, n - 1, S)), pltpu.SemaphoreType.DMA((2, n - 1, S))],
        compiler_params=pltpu.CompilerParams(collective_id=cid, has_side_effects=True, vmem_limit_bytes=32 << 20), name="rs")(p)

def ffn_kernel(
    n, axis, own_ref, go_ref, w_ref, gb_ref, part_ref, gw_ref,
    branch, wbuf, act, gpart, rb, w_sem, out_sem, send_ag, recv_ag, send_rs, recv_rs,
):
    me = lax.axis_index(axis)
    rows_own, width = own_ref.shape
    hidden = wbuf.shape[2]
    cut = hidden // 3
    wcut = width // 4
    loads = [
        pltpu.make_async_copy(w_ref.at[:, pl.ds(m * hidden, hidden)], wbuf.at[m], w_sem.at[m])
        for m in range(3)
    ]
    for load in loads:
        load.start()
    greet(me, n, axis)

    def block(j):
        return pl.ds(pl.multiple_of(j * rows_own, rows_own), rows_own)

    def passing(di, d, k, sender):
        j = sender - d * k
        return pltpu.make_async_remote_copy(
            src_ref=branch.at[block(j)], dst_ref=branch.at[block(j)],
            send_sem=send_ag.at[di, k], recv_sem=recv_ag.at[di, k],
            device_id={axis: sender + d}, device_id_type=MESH,
        )

    def first_pass(di, d):
        return pltpu.make_async_remote_copy(
            src_ref=own_ref, dst_ref=branch.at[block(me)],
            send_sem=send_ag.at[di, 0], recv_sem=recv_ag.at[di, 0],
            device_id={axis: me + d}, device_id_type=MESH,
        )

    sides = ((0, 1), (1, -1))
    for di, d in sides:
        @pl.when(inside(me + d, n))
        def _():
            first_pass(di, d).start()
    branch[block(me), :] = own_ref[...]
    for load in loads:
        load.wait()

    def chunk(j):
        at = block(j)
        for f in range(3):
            cols = pl.ds(f * cut, cut)
            gate = jnp.dot(branch[at, :], wbuf[0, :, cols], preferred_element_type=jnp.float32)
            upward = jnp.dot(branch[at, :], wbuf[1, :, cols], preferred_element_type=jnp.float32)
            sig = jax.nn.sigmoid(gate)
            silu = gate * sig
            act[2, at, cols] = (silu * upward).astype(jnp.bfloat16)
            gprod = jnp.dot(go_ref[at, :], wbuf[2, :, cols], preferred_element_type=jnp.float32)
            act[0, at, cols] = (gprod * upward * (sig * (1.0 + gate * (1.0 - sig)))).astype(jnp.bfloat16)
            act[1, at, cols] = (gprod * silu).astype(jnp.bfloat16)
        for f in range(4):
            cols = pl.ds(f * wcut, wcut)
            part_ref[at, cols] = dot_t(act[2, at, :], wbuf[2, cols, :]).astype(jnp.bfloat16)
            gpart[at, cols] = (
                dot_t(act[0, at, :], wbuf[0, cols, :]) + dot_t(act[1, at, :], wbuf[1, cols, :])
            ).astype(jnp.bfloat16)

    def distance(k, carry):
        for di, d in sides:
            @pl.when((k > 0) & inside(me - d * k, n))
            def _():
                passing(di, d, k - 1, me - d).wait_recv()
                @pl.when(inside(me + d, n))
                def _():
                    passing(di, d, k, me).start()
        low = inside(me - k, n)
        high = (k > 0) & inside(me + k, n)
        number = low.astype(jnp.int32) + high.astype(jnp.int32)

        def one(i, c):
            j = jnp.where((i == 0) & low, me - k, me + k)
            chunk(j)
            return c

        lax.fori_loop(0, number, one, 0)
        return carry

    lax.fori_loop(0, n, distance, 0)

    def owner(d, q):
        return n - 1 - q if d > 0 else q

    def item(di, d, q, sender, first):
        src = gpart.at[block(owner(d, q))] if first else rb.at[di, q]
        return pltpu.make_async_remote_copy(
            src_ref=src, dst_ref=rb.at[di, q], send_sem=send_rs.at[di, q], recv_sem=recv_rs.at[di, q],
            device_id={axis: sender + d}, device_id_type=MESH,
        )

    ways = ((0, 1, me), (1, -1, n - 1 - me))
    for q in range(n - 1):
        for di, d, dist in ways:
            @pl.when(dist == 0)
            def _():
                item(di, d, q, me, True).start()

    tile = width // 4

    def leave(m, r):
        return pltpu.make_async_copy(
            wbuf.at[m, pl.ds(pl.multiple_of(r * tile, tile), tile)],
            gw_ref.at[pl.ds(pl.multiple_of(r * tile, tile), tile), pl.ds(m * hidden, hidden)],
            out_sem.at[m, r],
        )

    def weights(m, left):
        def one(r, c):
            at = pl.ds(pl.multiple_of(r * tile, tile), tile)
            wbuf[m, at, :] = lax.dot_general(
                left[:, at], act[m], (((0,), (0,)), ((), ())), preferred_element_type=jnp.float32
            ).astype(jnp.bfloat16)
            leave(m, r).start()
            return c

        lax.fori_loop(0, 4, one, 0)

    todo = [(2, go_ref), (0, branch), (1, branch)]
    for t in range(1, n):
        if todo:
            weights(*todo.pop(0))
        if t == n - 1:
            while todo:
                weights(*todo.pop(0))
            break
        for di, d, dist in ways:
            @pl.when((dist > 0) & (t >= dist))
            def _():
                q = t - dist
                item(di, d, q, me - d, False).wait_recv()
                rb[di, q] = (rb[di, q].astype(jnp.float32) + gpart[block(owner(d, q)), :].astype(jnp.float32)).astype(rb.dtype)
                item(di, d, q, me, False).start()
    for di, d, dist in ways:
        @pl.when(dist > 0)
        def _():
            item(di, d, n - 1 - dist, me - d, False).wait_recv()
    @pl.when(me == 0)
    def _():
        gb_ref[...] = gpart[block(0), :].astype(jnp.float32) + rb[1, 0].astype(jnp.float32)
    @pl.when(me == n - 1)
    def _():
        gb_ref[...] = gpart[block(n - 1), :].astype(jnp.float32) + rb[0, 0].astype(jnp.float32)
    @pl.when((me > 0) & (me < n - 1))
    def _():
        gb_ref[...] = gpart[block(me), :].astype(jnp.float32) + rb[0, n - 1 - me].astype(jnp.float32) + rb[1, me].astype(jnp.float32)

    for k in range(n - 1):
        for di, d in sides:
            @pl.when(inside(me - d * k, n) & inside(me + d, n))
            def _():
                passing(di, d, k, me).wait_send()
    for t in range(n - 1):
        for di, d, dist in ways:
            @pl.when(t >= dist)
            def _():
                item(di, d, t - dist, me, False).wait_send()
    for m in range(3):
        for r in range(4):
            leave(m, r).wait()


def dot_t(left, right):
    return lax.dot_general(left, right, (((1,), (1,)), ((), ())), preferred_element_type=jnp.float32)


def ffn(own, go, w, n, cid, axis="tp"):
    rows_own, width = own.shape
    total = rows_own * n
    hidden = w.shape[1] // 3
    vmem = pl.BlockSpec(memory_space=pltpu.VMEM)
    any_space = pl.BlockSpec(memory_space=pl.ANY)
    dma = pltpu.SemaphoreType.DMA
    return pl.pallas_call(
        functools.partial(ffn_kernel, n, axis),
        out_shape=(
            jax.ShapeDtypeStruct((rows_own, width), jnp.float32),
            jax.ShapeDtypeStruct((total, width), jnp.bfloat16),
            jax.ShapeDtypeStruct(w.shape, jnp.bfloat16),
        ),
        in_specs=[vmem, vmem, any_space],
        out_specs=(vmem, vmem, any_space),
        scratch_shapes=[
            pltpu.VMEM((total, width), jnp.bfloat16),
            pltpu.VMEM((3, width, hidden), jnp.bfloat16),
            pltpu.VMEM((3, total, hidden), jnp.bfloat16),
            pltpu.VMEM((total, width), jnp.bfloat16),
            pltpu.VMEM((2, n - 1, rows_own, width), jnp.bfloat16),
            dma((3,)), dma((3, 4)), dma((2, n - 1)), dma((2, n - 1)), dma((2, n - 1)), dma((2, n - 1)),
        ],
        compiler_params=pltpu.CompilerParams(
            collective_id=cid, has_side_effects=True, vmem_limit_bytes=VMEM_LIMIT
        ),
        cost_estimate=pl.CostEstimate(
            flops=18 * total * width * hidden, bytes_accessed=12 * width * hidden, transcendentals=0
        ),
        name="ffn",
    )(own, go, w)


def per_device(
    hidden_in,
    grad_out,
    prefix_len,
    positions,
    g_attn,
    w_query,
    w_key,
    w_value,
    w_out,
    q_gain,
    k_gain,
    g_ffn,
    w_gate,
    w_up,
    w_down,
):
    parts = lax.axis_size("tp")
    groups = lax.axis_size("fsdp")
    own_rows, width = hidden_in.shape
    group_rows = own_rows * parts
    count = prefix_len.shape[0]
    length = group_rows // count
    qc, kc, fc = w_query.shape[1], w_key.shape[1], w_gate.shape[1]
    slot = g_attn.shape[0]
    head_slot = q_gain.shape[0]
    packed = jnp.concatenate([g_attn, g_ffn, q_gain, k_gain])[None]
    gains = lax.all_gather(packed, "fsdp", axis=0, tiled=True).astype(jnp.float32)
    first_gain = gains[:, :slot].reshape(-1)
    second_gain = gains[:, slot : 2 * slot].reshape(-1)
    query_gain = gains[:, 2 * slot : 2 * slot + head_slot].reshape(-1)
    key_gain = gains[:, 2 * slot + head_slot :].reshape(-1)
    attn_set = lax.all_gather(
        jnp.concatenate([w_query, w_key, w_value, w_out.T], axis=1), "fsdp", axis=0, tiled=True
    )
    full_qkv = attn_set[:, : qc + 2 * kc]
    full_out = attn_set[:, qc + 2 * kc :]
    ffn_set = lax.all_gather(
        jnp.concatenate([w_gate, w_up, w_down.T], axis=1), "fsdp", axis=0, tiled=True
    )

    tokens_all = ag(hidden_in, parts, cid=1)
    tokens_float = tokens_all.astype(jnp.float32)
    own_float = hidden_in.astype(jnp.float32)
    normed = norm_gain(tokens_float, first_gain).astype(jnp.bfloat16)
    raw = jnp.dot(normed, full_qkv, preferred_element_type=jnp.float32)
    query_raw = raw[:, :qc].reshape(group_rows, -1, HD)
    keys_raw = raw[:, qc : qc + kc].reshape(group_rows, -1, HD)
    values_low = raw[:, qc + kc :].astype(jnp.bfloat16).reshape(group_rows, -1, HD)
    kv_local = keys_raw.shape[1]
    grouping = query_raw.shape[1] // kv_local
    cosine, sine = rope_tables(positions)
    query_low = head_prep(query_raw, query_gain, cosine, sine).astype(jnp.bfloat16)
    keys_low = head_prep(keys_raw, key_gain, cosine, sine).astype(jnp.bfloat16)
    query_seq = query_low.reshape(count, length, kv_local, grouping, HD)
    keys_seq = keys_low.reshape(count, length, kv_local, HD)
    values_seq = values_low.reshape(count, length, kv_local, HD)
    mixed, log_total = lax.map(attend_forward, (query_seq, keys_seq, values_seq, prefix_len))
    mixed_low = mixed.reshape(group_rows, -1).astype(jnp.bfloat16)
    attn_part = jnp.einsum("th,dh->td", mixed_low, full_out, preferred_element_type=jnp.float32)
    middle = own_float + rs(attn_part.astype(jnp.bfloat16), parts, cid=2)
    grad_held, unused_tokens = lax.optimization_barrier((grad_out, tokens_all))
    grad_all = lax.all_gather(grad_held, "tp", axis=0, tiled=True)
    branch_own = norm_gain(middle, second_gain).astype(jnp.bfloat16)
    grad_branch_own, ffn_part, grad_w_ffn = ffn(branch_own, grad_all, ffn_set, parts, cid=3)
    result = middle + lax.psum_scatter(
        ffn_part, "tp", scatter_dimension=0, tiled=True
    ).astype(jnp.float32)
    out = result.astype(jnp.bfloat16)
    unused_second, pull_second = jax.vjp(norm_gain, middle, second_gain)
    grad_mid_norm, grad_second = pull_second(grad_branch_own)
    grad_middle = grad_out.astype(jnp.float32) + grad_mid_norm
    grad_mid_all = ag(grad_middle.astype(jnp.bfloat16), parts, cid=5)

    def spread(value):
        return lax.psum_scatter(
            value.astype(jnp.bfloat16), "fsdp", scatter_dimension=0, tiled=True
        ).astype(jnp.float32)

    ffn_own = spread(grad_w_ffn)
    grad_mixed = jnp.dot(grad_mid_all, full_out, preferred_element_type=jnp.float32).astype(
        jnp.bfloat16
    )
    grad_w_out = jnp.einsum(
        "td,th->dh", grad_mid_all, mixed_low, preferred_element_type=jnp.float32
    )
    grad_mixed_seq = grad_mixed.reshape(count, length, kv_local, grouping, HD)
    grads_query, grads_keys, grads_values = lax.map(
        attend_backward, (query_seq, keys_seq, values_seq, grad_mixed_seq, log_total, prefix_len)
    )
    unused_query, pull_query = jax.vjp(
        functools.partial(head_prep, cosine=cosine, sine=sine), query_raw, query_gain
    )
    grad_query_raw, grad_q_gain = pull_query(grads_query.reshape(group_rows, -1, HD))
    unused_keys, pull_keys = jax.vjp(
        functools.partial(head_prep, cosine=cosine, sine=sine), keys_raw, key_gain
    )
    grad_keys_raw, grad_k_gain = pull_keys(grads_keys.reshape(group_rows, -1, HD))
    grad_qkv = jnp.concatenate(
        [
            grad_query_raw.reshape(group_rows, -1),
            grad_keys_raw.reshape(group_rows, -1),
            grads_values.reshape(group_rows, -1),
        ],
        axis=1,
    ).astype(jnp.bfloat16)
    grad_w_qkv = jnp.einsum("td,th->dh", normed, grad_qkv, preferred_element_type=jnp.float32)
    grad_normed = jnp.einsum("th,dh->td", grad_qkv, full_qkv, preferred_element_type=jnp.float32)
    out_own = spread(grad_w_out)
    qkv_own = spread(grad_w_qkv)
    grad_normed_own = rs(grad_normed.astype(jnp.bfloat16), parts, cid=6)
    unused_first, pull_first = jax.vjp(norm_gain, own_float, first_gain)
    grad_tokens, grad_first = pull_first(grad_normed_own)
    grad_in = grad_middle + grad_tokens
    sums = lax.psum(
        jnp.concatenate([grad_first, grad_second, grad_q_gain, grad_k_gain]), ("fsdp", "tp")
    )
    place = lax.axis_index("fsdp")
    wide = groups * slot
    narrow = groups * head_slot
    gain_first = lax.dynamic_slice_in_dim(sums, place * slot, slot)
    gain_second = lax.dynamic_slice_in_dim(sums, wide + place * slot, slot)
    gain_query = lax.dynamic_slice_in_dim(sums, 2 * wide + place * head_slot, head_slot)
    gain_key = lax.dynamic_slice_in_dim(sums, 2 * wide + narrow + place * head_slot, head_slot)
    return (
        out,
        grad_in,
        gain_first,
        qkv_own[:, :qc],
        qkv_own[:, qc : qc + kc],
        qkv_own[:, qc + kc :],
        out_own.T,
        gain_query,
        gain_key,
        gain_second,
        ffn_own[:, :fc],
        ffn_own[:, fc : 2 * fc],
        ffn_own[:, 2 * fc :].T,
    )


def solution(mesh):
    in_specs = (
        P(("fsdp", "tp"), None),
        P(("fsdp", "tp"), None),
        P("fsdp"),
        P("fsdp"),
        P("fsdp"),
        P("fsdp", "tp"),
        P("fsdp", "tp"),
        P("fsdp", "tp"),
        P("tp", "fsdp"),
        P("fsdp"),
        P("fsdp"),
        P("fsdp"),
        P("fsdp", "tp"),
        P("fsdp", "tp"),
        P("tp", "fsdp"),
    )
    out_specs = (
        P(("fsdp", "tp"), None),
        P(("fsdp", "tp"), None),
        P("fsdp"),
        P("fsdp", "tp"),
        P("fsdp", "tp"),
        P("fsdp", "tp"),
        P("tp", "fsdp"),
        P("fsdp"),
        P("fsdp"),
        P("fsdp"),
        P("fsdp", "tp"),
        P("fsdp", "tp"),
        P("tp", "fsdp"),
    )
    return jax.shard_map(
        per_device, mesh=mesh, in_specs=in_specs, out_specs=out_specs, check_vma=False
    )
```

```python
import functools
import math

import jax
import jax.numpy as jnp
from jax import lax
from jax.experimental import pallas as pl
from jax.experimental.pallas import tpu as pltpu
from jax.sharding import PartitionSpec as P

MESH = pl.DeviceIdType.MESH
VMEM_LIMIT = 67043328

HD = 128


EPS = 1e-06
ROPE_BASE = 1000000.0


def rms_scale(value):
    return lax.rsqrt(jnp.mean(value * value, axis=-1, keepdims=True) + EPS)


def norm_gain(value, gain):
    return value * rms_scale(value) * gain


def rope_tables(places):
    half = HD // 2
    ladder = jnp.arange(half, dtype=jnp.float32) * (2.0 / HD)
    frequency = jnp.exp(-ladder * math.log(ROPE_BASE))
    angle = places.astype(jnp.float32)[:, None] * frequency[None, :]
    return (jnp.cos(angle)[:, None, :], jnp.sin(angle)[:, None, :])


def rotate(value, cosine, sine):
    half = value.shape[-1] // 2
    first = value[..., :half]
    second = value[..., half:]
    return jnp.concatenate(
        [first * cosine - second * sine, second * cosine + first * sine], axis=-1
    )


def head_prep(raw, gain, cosine, sine):
    return rotate(norm_gain(raw, gain), cosine, sine)


def visibility(length, prefix):
    places = jnp.arange(length, dtype=jnp.int32)
    return (places[None, :] <= places[:, None]) | (places[None, :] < prefix)


def masked_scores(query, keys, prefix):
    scale = 1.0 / math.sqrt(HD)
    scores = jnp.einsum("qkgd,pkd->kgqp", query, keys, preferred_element_type=jnp.float32) * scale
    return jnp.where(visibility(query.shape[0], prefix), scores, -1e30)


def attend_forward(item):
    query, keys, values, prefix = item
    scores = masked_scores(query, keys, prefix)
    peak = jnp.max(scores, axis=-1, keepdims=True)
    raised = jnp.exp(scores - peak)
    total = jnp.sum(raised, axis=-1, keepdims=True)
    shares = raised / total
    mixed = jnp.einsum(
        "kgqp,pkd->qkgd", shares.astype(jnp.bfloat16), values, preferred_element_type=jnp.float32
    )
    return (mixed, (peak + jnp.log(total))[..., 0])


def greet(me, n, axis):
    barrier = pltpu.get_barrier_semaphore()
    for d in (1, -1):
        @pl.when((me + d >= 0) & (me + d < n))
        def _():
            pl.semaphore_signal(barrier, inc=1, device_id={axis: me + d}, device_id_type=MESH)
    edge = (me == 0) | (me == n - 1)

    @pl.when(edge)
    def _():
        pl.semaphore_wait(barrier, 1)

    @pl.when(~edge)
    def _():
        pl.semaphore_wait(barrier, 2)

def inside(v, n):
    return (v >= 0) & (v < n)

def ag_kernel(n, S, axis, x_ref, o_ref, send_sem, recv_sem):
    me = lax.axis_index(axis)
    R = x_ref.shape[0]; sub = R // S
    greet(me, n, axis)
    def rows(j, s):
        return pl.ds(pl.multiple_of(j * R + s * sub, sub), sub)
    def item(di, d, k, s, sender):
        j = sender - d * k
        src = x_ref.at[pl.ds(s * sub, sub)] if k == 0 else o_ref.at[rows(j, s)]
        return pltpu.make_async_remote_copy(src_ref=src, dst_ref=o_ref.at[rows(j, s)], send_sem=send_sem.at[di, k, s], recv_sem=recv_sem.at[di, k, s], device_id={axis: sender + d}, device_id_type=MESH)
    for k in range(n):
        for s in range(S):
            for di, d in enumerate((1, -1)):
                if k > 0:
                    @pl.when(inside(me - d * k, n))
                    def _():
                        item(di, d, k - 1, s, me - d).wait_recv()
                if k < n - 1:
                    @pl.when(inside(me - d * k, n) & inside(me + d, n))
                    def _():
                        item(di, d, k, s, me).start()
        if k == 0:
            o_ref[pl.ds(pl.multiple_of(me * R, R), R), :] = x_ref[...]
    for k in range(n - 1):
        for s in range(S):
            for di, d in enumerate((1, -1)):
                @pl.when(inside(me - d * k, n) & inside(me + d, n))
                def _():
                    item(di, d, k, s, me).wait_send()

def ag(x, n, S=2, axis="tp", cid=1):
    R, D = x.shape
    return pl.pallas_call(functools.partial(ag_kernel, n, S, axis),
        out_shape=jax.ShapeDtypeStruct((n * R, D), x.dtype),
        in_specs=[pl.BlockSpec(memory_space=pltpu.VMEM)],
        out_specs=pl.BlockSpec(memory_space=pltpu.VMEM),
        scratch_shapes=[pltpu.SemaphoreType.DMA((2, n - 1, S)), pltpu.SemaphoreType.DMA((2, n - 1, S))],
        compiler_params=pltpu.CompilerParams(collective_id=cid, has_side_effects=True, vmem_limit_bytes=32 << 20), name="ag")(x)

def rs_kernel(n, S, axis, p_ref, o_ref, rb, send_sem, recv_sem):
    me = lax.axis_index(axis)
    R = o_ref.shape[0]; sub = R // S
    greet(me, n, axis)
    def rows(j, s):
        return pl.ds(pl.multiple_of(j * R + s * sub, sub), sub)
    def at(s):
        return pl.ds(s * sub, sub)
    def owner(d, q):
        return n - 1 - q if d > 0 else q
    def item(di, d, q, s, sender, first):
        src = p_ref.at[rows(owner(d, q), s)] if first else rb.at[di, q, at(s)]
        return pltpu.make_async_remote_copy(src_ref=src, dst_ref=rb.at[di, q, at(s)], send_sem=send_sem.at[di, q, s], recv_sem=recv_sem.at[di, q, s], device_id={axis: sender + d}, device_id_type=MESH)
    ways = ((0, 1, me), (1, -1, n - 1 - me))
    for q in range(n - 1):
        for s in range(S):
            for di, d, dist in ways:
                @pl.when(dist == 0)
                def _():
                    item(di, d, q, s, me, True).start()
    for t in range(1, n - 1):
        for s in range(S):
            for di, d, dist in ways:
                @pl.when((dist > 0) & (t >= dist))
                def _():
                    q = t - dist
                    item(di, d, q, s, me - d, False).wait_recv()
                    rb[di, q, at(s), :] = (rb[di, q, at(s), :].astype(jnp.float32) + p_ref[rows(owner(d, q), s), :].astype(jnp.float32)).astype(rb.dtype)
                    item(di, d, q, s, me, False).start()
    for s in range(S):
        for di, d, dist in ways:
            @pl.when(dist > 0)
            def _():
                item(di, d, n - 1 - dist, s, me - d, False).wait_recv()
        @pl.when(me == 0)
        def _():
            o_ref[at(s), :] = p_ref[rows(0, s), :].astype(jnp.float32) + rb[1, 0, at(s), :].astype(jnp.float32)
        @pl.when(me == n - 1)
        def _():
            o_ref[at(s), :] = p_ref[rows(n - 1, s), :].astype(jnp.float32) + rb[0, 0, at(s), :].astype(jnp.float32)
        @pl.when((me > 0) & (me < n - 1))
        def _():
            o_ref[at(s), :] = p_ref[rows(me, s), :].astype(jnp.float32) + rb[0, n - 1 - me, at(s), :].astype(jnp.float32) + rb[1, me, at(s), :].astype(jnp.float32)
    for t in range(0, n - 1):
        for s in range(S):
            for di, d, dist in ways:
                @pl.when(t >= dist)
                def _():
                    item(di, d, t - dist, s, me, False).wait_send()

def rs(p, n, S=2, axis="tp", cid=2):
    NR, D = p.shape; R = NR // n
    return pl.pallas_call(functools.partial(rs_kernel, n, S, axis),
        out_shape=jax.ShapeDtypeStruct((R, D), jnp.float32),
        in_specs=[pl.BlockSpec(memory_space=pltpu.VMEM)],
        out_specs=pl.BlockSpec(memory_space=pltpu.VMEM),
        scratch_shapes=[pltpu.VMEM((2, n - 1, R, D), p.dtype), pltpu.SemaphoreType.DMA((2, n - 1, S)), pltpu.SemaphoreType.DMA((2, n - 1, S))],
        compiler_params=pltpu.CompilerParams(collective_id=cid, has_side_effects=True, vmem_limit_bytes=32 << 20), name="rs")(p)

def ffn_kernel(
    n, axis, mid_ref, gain_ref, go_ref, w_ref, gmid_ref, gffn_ref, part_ref, gw_ref,
    branch, wbuf, act, gpart, rb, w_sem, out_sem, send_ag, recv_ag, send_rs, recv_rs,
):
    me = lax.axis_index(axis)
    rows_own, width = mid_ref.shape
    hidden = wbuf.shape[2]
    cut = hidden // 3
    wcut = width // 4
    loads = [
        pltpu.make_async_copy(w_ref.at[:, pl.ds(m * hidden, hidden)], wbuf.at[m], w_sem.at[m])
        for m in range(3)
    ]
    for load in loads:
        load.start()

    def block(j):
        return pl.ds(pl.multiple_of(j * rows_own, rows_own), rows_own)

    mid = mid_ref[...]
    inverse = lax.rsqrt(jnp.mean(mid * mid, axis=-1, keepdims=True) + EPS)
    branch[block(me), :] = (mid * inverse * gain_ref[...]).astype(jnp.bfloat16)
    greet(me, n, axis)

    def passing(di, d, k, sender):
        j = sender - d * k
        return pltpu.make_async_remote_copy(
            src_ref=branch.at[block(j)], dst_ref=branch.at[block(j)],
            send_sem=send_ag.at[di, k], recv_sem=recv_ag.at[di, k],
            device_id={axis: sender + d}, device_id_type=MESH,
        )

    sides = ((0, 1), (1, -1))
    for di, d in sides:
        @pl.when(inside(me + d, n))
        def _():
            passing(di, d, 0, me).start()
    for load in loads:
        load.wait()

    def chunk(j):
        at = block(j)
        for f in range(3):
            cols = pl.ds(f * cut, cut)
            gate = jnp.dot(branch[at, :], wbuf[0, :, cols], preferred_element_type=jnp.float32)
            upward = jnp.dot(branch[at, :], wbuf[1, :, cols], preferred_element_type=jnp.float32)
            sig = jax.nn.sigmoid(gate)
            silu = gate * sig
            act[2, at, cols] = (silu * upward).astype(jnp.bfloat16)
            gprod = jnp.dot(go_ref[at, :], wbuf[2, :, cols], preferred_element_type=jnp.float32)
            act[0, at, cols] = (gprod * upward * (sig * (1.0 + gate * (1.0 - sig)))).astype(jnp.bfloat16)
            act[1, at, cols] = (gprod * silu).astype(jnp.bfloat16)
        for f in range(4):
            cols = pl.ds(f * wcut, wcut)
            part_ref[at, cols] = dot_t(act[2, at, :], wbuf[2, cols, :]).astype(jnp.bfloat16)
            gpart[at, cols] = (
                dot_t(act[0, at, :], wbuf[0, cols, :]) + dot_t(act[1, at, :], wbuf[1, cols, :])
            ).astype(jnp.bfloat16)

    def distance(k, carry):
        for di, d in sides:
            @pl.when((k > 0) & inside(me - d * k, n))
            def _():
                passing(di, d, k - 1, me - d).wait_recv()
                @pl.when(inside(me + d, n))
                def _():
                    passing(di, d, k, me).start()
        low = inside(me - k, n)
        high = (k > 0) & inside(me + k, n)
        number = low.astype(jnp.int32) + high.astype(jnp.int32)

        def one(i, c):
            j = jnp.where((i == 0) & low, me - k, me + k)
            chunk(j)
            return c

        lax.fori_loop(0, number, one, 0)
        return carry

    lax.fori_loop(0, n, distance, 0)

    def owner(d, q):
        return n - 1 - q if d > 0 else q

    def item(di, d, q, sender, first):
        src = gpart.at[block(owner(d, q))] if first else rb.at[di, q]
        return pltpu.make_async_remote_copy(
            src_ref=src, dst_ref=rb.at[di, q], send_sem=send_rs.at[di, q], recv_sem=recv_rs.at[di, q],
            device_id={axis: sender + d}, device_id_type=MESH,
        )

    ways = ((0, 1, me), (1, -1, n - 1 - me))
    for q in range(n - 1):
        for di, d, dist in ways:
            @pl.when(dist == 0)
            def _():
                item(di, d, q, me, True).start()

    tile = width // 4

    def leave(m, r):
        return pltpu.make_async_copy(
            wbuf.at[m, pl.ds(pl.multiple_of(r * tile, tile), tile)],
            gw_ref.at[pl.ds(pl.multiple_of(r * tile, tile), tile), pl.ds(m * hidden, hidden)],
            out_sem.at[m, r],
        )

    def weights(m, left):
        def one(r, c):
            at = pl.ds(pl.multiple_of(r * tile, tile), tile)
            wbuf[m, at, :] = lax.dot_general(
                left[:, at], act[m], (((0,), (0,)), ((), ())), preferred_element_type=jnp.float32
            ).astype(jnp.bfloat16)
            leave(m, r).start()
            return c

        lax.fori_loop(0, 4, one, 0)

    todo = [(2, go_ref), (0, branch), (1, branch)]
    for t in range(1, n):
        if todo:
            weights(*todo.pop(0))
        if t == n - 1:
            while todo:
                weights(*todo.pop(0))
            break
        for di, d, dist in ways:
            @pl.when((dist > 0) & (t >= dist))
            def _():
                q = t - dist
                item(di, d, q, me - d, False).wait_recv()
                rb[di, q] = (rb[di, q].astype(jnp.float32) + gpart[block(owner(d, q)), :].astype(jnp.float32)).astype(rb.dtype)
                item(di, d, q, me, False).start()
    for di, d, dist in ways:
        @pl.when(dist > 0)
        def _():
            item(di, d, n - 1 - dist, me - d, False).wait_recv()
    @pl.when(me == 0)
    def _():
        gmid_ref[...] = gpart[block(0), :].astype(jnp.float32) + rb[1, 0].astype(jnp.float32)
    @pl.when(me == n - 1)
    def _():
        gmid_ref[...] = gpart[block(n - 1), :].astype(jnp.float32) + rb[0, 0].astype(jnp.float32)
    @pl.when((me > 0) & (me < n - 1))
    def _():
        gmid_ref[...] = gpart[block(me), :].astype(jnp.float32) + rb[0, n - 1 - me].astype(jnp.float32) + rb[1, me].astype(jnp.float32)
    mid = mid_ref[...]
    inverse = lax.rsqrt(jnp.mean(mid * mid, axis=-1, keepdims=True) + EPS)
    unit = mid * inverse
    grad = gmid_ref[...]
    gffn_ref[...] = jnp.sum(grad * unit, axis=0, keepdims=True)
    scaled = grad * gain_ref[...]
    gmid_ref[...] = go_ref[block(me), :].astype(jnp.float32) + inverse * (scaled - unit * jnp.mean(scaled * unit, axis=-1, keepdims=True))

    for k in range(n - 1):
        for di, d in sides:
            @pl.when(inside(me - d * k, n) & inside(me + d, n))
            def _():
                passing(di, d, k, me).wait_send()
    for t in range(n - 1):
        for di, d, dist in ways:
            @pl.when(t >= dist)
            def _():
                item(di, d, t - dist, me, False).wait_send()
    for m in range(3):
        for r in range(4):
            leave(m, r).wait()


def dot_t(left, right):
    return lax.dot_general(left, right, (((1,), (1,)), ((), ())), preferred_element_type=jnp.float32)


def ffn(mid, gain, go, w, n, cid, axis="tp"):
    rows_own, width = mid.shape
    total = rows_own * n
    hidden = w.shape[1] // 3
    vmem = pl.BlockSpec(memory_space=pltpu.VMEM)
    any_space = pl.BlockSpec(memory_space=pl.ANY)
    dma = pltpu.SemaphoreType.DMA
    return pl.pallas_call(
        functools.partial(ffn_kernel, n, axis),
        out_shape=(
            jax.ShapeDtypeStruct((rows_own, width), jnp.float32),
            jax.ShapeDtypeStruct((1, width), jnp.float32),
            jax.ShapeDtypeStruct((total, width), jnp.bfloat16),
            jax.ShapeDtypeStruct(w.shape, jnp.bfloat16),
        ),
        in_specs=[vmem, vmem, vmem, any_space],
        out_specs=(vmem, vmem, vmem, any_space),
        scratch_shapes=[
            pltpu.VMEM((total, width), jnp.bfloat16),
            pltpu.VMEM((3, width, hidden), jnp.bfloat16),
            pltpu.VMEM((3, total, hidden), jnp.bfloat16),
            pltpu.VMEM((total, width), jnp.bfloat16),
            pltpu.VMEM((2, n - 1, rows_own, width), jnp.bfloat16),
            dma((3,)), dma((3, 4)), dma((2, n - 1)), dma((2, n - 1)), dma((2, n - 1)), dma((2, n - 1)),
        ],
        compiler_params=pltpu.CompilerParams(
            collective_id=cid, has_side_effects=True, vmem_limit_bytes=VMEM_LIMIT
        ),
        cost_estimate=pl.CostEstimate(
            flops=18 * total * width * hidden, bytes_accessed=12 * width * hidden, transcendentals=0
        ),
        name="ffn",
    )(mid, gain, go, w)


def exchange_plan(n, me):
    return ((0, 1, me), (1, -1, n - 1 - me))


def unroll_rot(value, cos2, sin2):
    return value * cos2 - pltpu.roll(value, HD // 2, 1) * sin2


def attn_back_kernel(
    n, axis, heads, kv_heads,
    gmid_ref, mid_ref, cos_ref, sin_ref, lse_ref, gain_ref, prefix_ref,
    w_hbm, normed_hbm, qkv_hbm, raw_hbm, mixed_hbm, part_hbm,
    out_ref, gn_ref, gsum_ref, gw_ref,
    wbuf, normed, qkv, raw, mixed, part, gm, gmix, keys_t, dk, dv, gqkv, rb,
    load_sem, out_sem, send_ag, recv_ag, send_rs, recv_rs,
):
    me = lax.axis_index(axis)
    rows_own, width = gmid_ref.shape
    total = rows_own * n
    qc, kc = heads * HD, kv_heads * HD
    group = heads // kv_heads
    scale = 1.0 / math.sqrt(HD)
    pairs = ((w_hbm, wbuf), (qkv_hbm, qkv), (raw_hbm, raw), (part_hbm, part), (normed_hbm, normed), (mixed_hbm, mixed))
    loads = [pltpu.make_async_copy(src, dst, load_sem.at[i]) for i, (src, dst) in enumerate(pairs)]
    for load in loads:
        load.start()

    def block(j):
        return pl.ds(pl.multiple_of(j * rows_own, rows_own), rows_own)

    gm[block(me), :] = gmid_ref[...].astype(jnp.bfloat16)
    dk[...] = jnp.zeros_like(dk)
    dv[...] = jnp.zeros_like(dv)
    gsum_ref[...] = jnp.zeros_like(gsum_ref)
    greet(me, n, axis)

    def passing(di, d, k, sender):
        j = sender - d * k
        return pltpu.make_async_remote_copy(
            src_ref=gm.at[block(j)], dst_ref=gm.at[block(j)],
            send_sem=send_ag.at[di, k], recv_sem=recv_ag.at[di, k],
            device_id={axis: sender + d}, device_id_type=MESH,
        )

    def owner(d, q):
        return n - 1 - q if d > 0 else q

    def item(di, d, q, sender, first):
        src = part.at[block(owner(d, q))] if first else rb.at[di, q]
        return pltpu.make_async_remote_copy(
            src_ref=src, dst_ref=rb.at[di, q], send_sem=send_rs.at[di, q], recv_sem=recv_rs.at[di, q],
            device_id={axis: sender + d}, device_id_type=MESH,
        )

    sides = ((0, 1), (1, -1))
    ways = exchange_plan(n, me)
    for di, d in sides:
        @pl.when(inside(me + d, n))
        def _():
            passing(di, d, 0, me).start()
    for load in loads[:3]:
        load.wait()
    for g in range(kv_heads):
        keys_t[g] = qkv[:, qc + g * HD : qc + (g + 1) * HD].T
    loads[3].wait()
    prefix = prefix_ref[0]

    def unit_of(at, first):
        value = raw[at, first : first + HD]
        inverse = lax.rsqrt(jnp.mean(value * value, axis=-1, keepdims=True) + EPS)
        return value * inverse, inverse

    def normed_back(grad, at, first, gain, place):
        unit, inverse = unit_of(at, first)
        turned = unroll_rot(grad, cos_ref[at, :], sin_ref[at, :])
        gsum_ref[place : place + 1, :] += jnp.sum(turned * unit, axis=0, keepdims=True)
        scaled = turned * gain
        return (inverse * (scaled - unit * jnp.mean(scaled * unit, axis=-1, keepdims=True))).astype(jnp.bfloat16)

    def chunk(j):
        at = block(j)
        gmix[...] = jnp.dot(gm[at, :], wbuf[:, qc + 2 * kc :], preferred_element_type=jnp.float32).astype(jnp.bfloat16)
        key_at = lax.broadcasted_iota(jnp.int32, (total, rows_own), 0)
        query_at = lax.broadcasted_iota(jnp.int32, (total, rows_own), 1) + j * rows_own
        seen = (key_at <= query_at) | (key_at < prefix)
        for h in range(heads):
            g = h // group
            ks, vs, hs = qc + g * HD, qc + kc + g * HD, h * HD
            q = qkv[at, hs : hs + HD]
            gx = gmix[:, hs : hs + HD]
            scores = dot_t(qkv[:, ks : ks + HD], q) * scale
            shares = jnp.where(seen, jnp.exp(scores - lse_ref[h : h + 1, at]), 0.0)
            grad_shares = dot_t(qkv[:, vs : vs + HD], gx)
            delta = jnp.sum(grad_shares * shares, axis=0, keepdims=True)
            low = (shares * (grad_shares - delta) * scale).astype(jnp.bfloat16)
            gcols = pl.ds(g * HD, HD)
            dk[:, gcols] += jnp.dot(low, q, preferred_element_type=jnp.float32)
            dv[:, gcols] += jnp.dot(shares.astype(jnp.bfloat16), gx, preferred_element_type=jnp.float32)
            dq = jnp.dot(keys_t[g], low, preferred_element_type=jnp.float32).T
            gqkv[at, hs : hs + HD] = normed_back(dq, at, hs, gain_ref[0:1, :], 0)

    def sums_step(t):
        for di, d, dist in ways:
            @pl.when((dist > 0) & (t >= dist))
            def _():
                q = t - dist
                item(di, d, q, me - d, False).wait_recv()
                rb[di, q] = (rb[di, q].astype(jnp.float32) + part[block(owner(d, q)), :].astype(jnp.float32)).astype(rb.dtype)
                item(di, d, q, me, False).start()

    def distance(k, carry):
        for di, d in sides:
            @pl.when((k > 0) & inside(me - d * k, n))
            def _():
                passing(di, d, k - 1, me - d).wait_recv()
                @pl.when(inside(me + d, n))
                def _():
                    passing(di, d, k, me).start()

        for di, d, dist in ways:
            @pl.when((k == 1) & (dist == 0))
            def _():
                for q in range(n - 1):
                    item(di, d, q, me, True).start()

        @pl.when(k > 1)
        def _():
            sums_step(k - 1)

        low = inside(me - k, n)
        high = (k > 0) & inside(me + k, n)
        number = low.astype(jnp.int32) + high.astype(jnp.int32)

        def one(i, c):
            chunk(jnp.where((i == 0) & low, me - k, me + k))
            return c

        lax.fori_loop(0, number, one, 0)
        return carry

    lax.fori_loop(0, n, distance, 0)

    for load in loads[4:]:
        load.wait()

    def finish(j, carry):
        at = block(j)
        for g in range(kv_heads):
            ks, vs = qc + g * HD, qc + kc + g * HD
            gqkv[at, ks : ks + HD] = normed_back(dk[at, g * HD : (g + 1) * HD], at, ks, gain_ref[1:2, :], 1)
            gqkv[at, vs : vs + HD] = dv[at, g * HD : (g + 1) * HD].astype(jnp.bfloat16)
        cut = width // 4
        for f in range(4):
            cols = pl.ds(f * cut, cut)
            gn_ref[at, cols] = dot_t(gqkv[at, :], wbuf[cols, : qc + 2 * kc]).astype(jnp.bfloat16)
        return carry

    lax.fori_loop(0, n, finish, 0)

    tile = width // 4

    def leave(r):
        at = pl.ds(pl.multiple_of(r * tile, tile), tile)
        return pltpu.make_async_copy(wbuf.at[at], gw_ref.at[at], out_sem.at[r])

    def weights(r, carry):
        at = pl.ds(pl.multiple_of(r * tile, tile), tile)
        wbuf[at, : qc + 2 * kc] = lax.dot_general(
            normed[:, at], gqkv[...], (((0,), (0,)), ((), ())), preferred_element_type=jnp.float32
        ).astype(jnp.bfloat16)
        wbuf[at, qc + 2 * kc :] = lax.dot_general(
            gm[:, at], mixed[...], (((0,), (0,)), ((), ())), preferred_element_type=jnp.float32
        ).astype(jnp.bfloat16)
        leave(r).start()
        return carry

    lax.fori_loop(0, 4, weights, 0)

    for di, d, dist in ways:
        @pl.when(dist > 0)
        def _():
            item(di, d, n - 1 - dist, me - d, False).wait_recv()
    own = mid_ref[...] + part[block(me), :].astype(jnp.float32)
    @pl.when(me == 0)
    def _():
        out_ref[...] = (own + rb[1, 0].astype(jnp.float32)).astype(out_ref.dtype)
    @pl.when(me == n - 1)
    def _():
        out_ref[...] = (own + rb[0, 0].astype(jnp.float32)).astype(out_ref.dtype)
    @pl.when((me > 0) & (me < n - 1))
    def _():
        out_ref[...] = (own + rb[0, n - 1 - me].astype(jnp.float32) + rb[1, me].astype(jnp.float32)).astype(out_ref.dtype)

    for k in range(n - 1):
        for di, d in sides:
            @pl.when(inside(me - d * k, n) & inside(me + d, n))
            def _():
                passing(di, d, k, me).wait_send()
    for t in range(n - 1):
        for di, d, dist in ways:
            @pl.when(t >= dist)
            def _():
                item(di, d, t - dist, me, False).wait_send()
    for r in range(4):
        leave(r).wait()


def attn_back(gmid, mid, cos2, sin2, lse, gains, prefix, w, normed, qkv, raw, mixed, part, n, heads, kv_heads, cid, axis="tp"):
    rows_own, width = gmid.shape
    total = rows_own * n
    vmem = pl.BlockSpec(memory_space=pltpu.VMEM)
    any_space = pl.BlockSpec(memory_space=pl.ANY)
    dma = pltpu.SemaphoreType.DMA
    return pl.pallas_call(
        functools.partial(attn_back_kernel, n, axis, heads, kv_heads),
        out_shape=(
            jax.ShapeDtypeStruct((rows_own, width), jnp.bfloat16),
            jax.ShapeDtypeStruct((total, width), jnp.bfloat16),
            jax.ShapeDtypeStruct((8, HD), jnp.float32),
            jax.ShapeDtypeStruct(w.shape, jnp.bfloat16),
        ),
        in_specs=[vmem] * 6 + [pl.BlockSpec(memory_space=pltpu.SMEM)] + [any_space] * 6,
        out_specs=(vmem, vmem, vmem, any_space),
        scratch_shapes=[
            pltpu.VMEM(w.shape, jnp.bfloat16),
            pltpu.VMEM(normed.shape, jnp.bfloat16),
            pltpu.VMEM(qkv.shape, jnp.bfloat16),
            pltpu.VMEM(raw.shape, jnp.float32),
            pltpu.VMEM(mixed.shape, jnp.bfloat16),
            pltpu.VMEM(part.shape, jnp.bfloat16),
            pltpu.VMEM((total, width), jnp.bfloat16),
            pltpu.VMEM((rows_own, heads * HD), jnp.bfloat16),
            pltpu.VMEM((kv_heads, HD, total), jnp.bfloat16),
            pltpu.VMEM((total, kv_heads * HD), jnp.float32),
            pltpu.VMEM((total, kv_heads * HD), jnp.float32),
            pltpu.VMEM(qkv.shape, jnp.bfloat16),
            pltpu.VMEM((2, n - 1, rows_own, width), jnp.bfloat16),
            dma((6,)), dma((4,)), dma((2, n - 1)), dma((2, n - 1)), dma((2, n - 1)), dma((2, n - 1)),
        ],
        compiler_params=pltpu.CompilerParams(
            collective_id=cid, has_side_effects=True, vmem_limit_bytes=VMEM_LIMIT
        ),
        cost_estimate=pl.CostEstimate(flops=30 * total * width * HD, bytes_accessed=40 * total * width, transcendentals=0),
        name="attn_back",
    )(gmid, mid, cos2, sin2, lse, gains, prefix, w, normed, qkv, raw, mixed, part)


def final_kernel(
    n, groups, p_ref, x_ref, gmid_ref, gain_ref, gffn_ref, small_ref, dx_ref, total_ref,
    rb, gsend, grecv, tsend, trecv, send_sem, recv_sem, gs_sem, gr_sem, ts_sem, tr_sem,
):
    me = lax.axis_index("tp")
    mine = lax.axis_index("fsdp")
    rows_own, width = dx_ref.shape
    slot = width // groups
    barrier = pltpu.get_barrier_semaphore()
    for f in range(groups):
        @pl.when(mine != f)
        def _():
            pl.semaphore_signal(barrier, inc=1, device_id={"fsdp": f}, device_id_type=MESH)
    for p in range(n):
        @pl.when(me != p)
        def _():
            pl.semaphore_signal(barrier, inc=1, device_id={"tp": p}, device_id_type=MESH)
    pl.semaphore_wait(barrier, groups + n - 2)

    def block(j):
        return pl.ds(pl.multiple_of(j * rows_own, rows_own), rows_own)

    def owner(d, q):
        return n - 1 - q if d > 0 else q

    halves = 2
    half = rows_own // halves

    def item(di, d, q, s, sender, first):
        at = pl.ds(s * half, half)
        src = p_ref.at[pl.ds(pl.multiple_of(owner(d, q) * rows_own + s * half, half), half)] if first else rb.at[di, q, at]
        return pltpu.make_async_remote_copy(
            src_ref=src, dst_ref=rb.at[di, q, at], send_sem=send_sem.at[di, q, s], recv_sem=recv_sem.at[di, q, s],
            device_id={"tp": sender + d}, device_id_type=MESH,
        )

    ways = exchange_plan(n, me)
    for q in range(n - 1):
        for s in range(halves):
            for di, d, dist in ways:
                @pl.when(dist == 0)
                def _():
                    item(di, d, q, s, me, True).start()
    for t in range(1, n - 1):
        for s in range(halves):
            for di, d, dist in ways:
                @pl.when((dist > 0) & (t >= dist))
                def _():
                    q = t - dist
                    at = pl.ds(s * half, half)
                    item(di, d, q, s, me - d, False).wait_recv()
                    mine_at = pl.ds(pl.multiple_of(owner(d, q) * rows_own + s * half, half), half)
                    rb[di, q, at, :] = (rb[di, q, at, :].astype(jnp.float32) + p_ref[mine_at, :].astype(jnp.float32)).astype(rb.dtype)
                    item(di, d, q, s, me, False).start()
    for s in range(halves):
        for di, d, dist in ways:
            @pl.when(dist > 0)
            def _():
                item(di, d, n - 1 - dist, s, me - d, False).wait_recv()
    own = p_ref[block(me), :].astype(jnp.float32)
    @pl.when(me == 0)
    def _():
        dx_ref[...] = own + rb[1, 0].astype(jnp.float32)
    @pl.when(me == n - 1)
    def _():
        dx_ref[...] = own + rb[0, 0].astype(jnp.float32)
    @pl.when((me > 0) & (me < n - 1))
    def _():
        dx_ref[...] = own + rb[0, n - 1 - me].astype(jnp.float32) + rb[1, me].astype(jnp.float32)

    x = x_ref[...].astype(jnp.float32)
    inverse = lax.rsqrt(jnp.mean(x * x, axis=-1, keepdims=True) + EPS)
    first = x * inverse
    grad = dx_ref[...]
    gattn = jnp.sum(grad * first, axis=0, keepdims=True)
    for f in range(groups):
        gsend[f, :, :slot] = gattn[:, f * slot : (f + 1) * slot]
        gsend[f, :, slot : 2 * slot] = gffn_ref[:, f * slot : (f + 1) * slot]
        gsend[f, :, 2 * slot : 2 * slot + HD] = small_ref[0:1, :]
        gsend[f, :, 2 * slot + HD :] = small_ref[1:2, :]

    def to_slot(f, sender):
        return pltpu.make_async_remote_copy(
            src_ref=gsend.at[f], dst_ref=grecv.at[sender], send_sem=gs_sem.at[f], recv_sem=gr_sem.at[sender],
            device_id={"fsdp": f}, device_id_type=MESH,
        )

    scaled = grad * gain_ref[...]
    dx_ref[...] = gmid_ref[...] + inverse * (scaled - first * jnp.mean(scaled * first, axis=-1, keepdims=True))
    for f in range(groups):
        @pl.when(mine != f)
        def _():
            to_slot(f, mine).start()
    grecv[mine] = gsend[mine]
    for f in range(groups):
        @pl.when(mine != f)
        def _():
            to_slot(f, f).wait_recv()
    tsend[...] = jnp.sum(grecv[...], axis=0)

    def to_part(p, sender):
        return pltpu.make_async_remote_copy(
            src_ref=tsend, dst_ref=trecv.at[sender], send_sem=ts_sem.at[p], recv_sem=tr_sem.at[sender],
            device_id={"tp": p}, device_id_type=MESH,
        )

    for p in range(n):
        @pl.when(me != p)
        def _():
            to_part(p, me).start()
    trecv[me] = tsend[...]
    for p in range(n):
        @pl.when(me != p)
        def _():
            to_part(p, p).wait_recv()
    total_ref[...] = jnp.sum(trecv[...], axis=0)
    for f in range(groups):
        @pl.when(mine != f)
        def _():
            to_slot(f, mine).wait_send()
    for p in range(n):
        @pl.when(me != p)
        def _():
            to_part(p, me).wait_send()
    for t in range(n - 1):
        for s in range(halves):
            for di, d, dist in ways:
                @pl.when(t >= dist)
                def _():
                    item(di, d, t - dist, s, me, False).wait_send()


def final(p, x, gmid, gain, gffn, small, n, groups, cid):
    rows_own, width = gmid.shape
    wide = 2 * (width // groups) + 2 * HD
    vmem = pl.BlockSpec(memory_space=pltpu.VMEM)
    dma = pltpu.SemaphoreType.DMA
    return pl.pallas_call(
        functools.partial(final_kernel, n, groups),
        out_shape=(
            jax.ShapeDtypeStruct((rows_own, width), jnp.float32),
            jax.ShapeDtypeStruct((1, wide), jnp.float32),
        ),
        in_specs=[vmem] * 6,
        out_specs=(vmem, vmem),
        scratch_shapes=[
            pltpu.VMEM((2, n - 1, rows_own, width), jnp.bfloat16),
            pltpu.VMEM((groups, 1, wide), jnp.float32),
            pltpu.VMEM((groups, 1, wide), jnp.float32),
            pltpu.VMEM((1, wide), jnp.float32),
            pltpu.VMEM((n, 1, wide), jnp.float32),
            dma((2, n - 1, 2)), dma((2, n - 1, 2)), dma((groups,)), dma((groups,)), dma((n,)), dma((n,)),
        ],
        compiler_params=pltpu.CompilerParams(
            collective_id=cid, has_side_effects=True, vmem_limit_bytes=40 << 20
        ),
        cost_estimate=pl.CostEstimate(flops=1 << 34, bytes_accessed=200 << 20, transcendentals=0),
        name="final",
    )(p, x, gmid, gain, gffn, small)


def per_device(
    hidden_in,
    grad_out,
    prefix_len,
    positions,
    g_attn,
    w_query,
    w_key,
    w_value,
    w_out,
    q_gain,
    k_gain,
    g_ffn,
    w_gate,
    w_up,
    w_down,
):
    parts = lax.axis_size("tp")
    groups = lax.axis_size("fsdp")
    own_rows, width = hidden_in.shape
    group_rows = own_rows * parts
    count = prefix_len.shape[0]
    length = group_rows // count
    qc, kc, fc = w_query.shape[1], w_key.shape[1], w_gate.shape[1]
    slot = g_attn.shape[0]
    head_slot = q_gain.shape[0]
    packed = jnp.concatenate([g_attn, g_ffn, q_gain, k_gain])[None]
    gains = lax.all_gather(packed, "fsdp", axis=0, tiled=True).astype(jnp.float32)
    first_gain = gains[:, :slot].reshape(-1)
    second_gain = gains[:, slot : 2 * slot].reshape(-1)
    query_gain = gains[:, 2 * slot : 2 * slot + head_slot].reshape(-1)
    key_gain = gains[:, 2 * slot + head_slot :].reshape(-1)
    attn_set = lax.all_gather(
        jnp.concatenate([w_query, w_key, w_value, w_out.T], axis=1), "fsdp", axis=0, tiled=True
    )
    full_qkv = attn_set[:, : qc + 2 * kc]
    full_out = attn_set[:, qc + 2 * kc :]
    ffn_set = lax.all_gather(
        jnp.concatenate([w_gate, w_up, w_down.T], axis=1), "fsdp", axis=0, tiled=True
    )

    tokens_all = ag(hidden_in, parts, cid=1)
    tokens_float = tokens_all.astype(jnp.float32)
    own_float = hidden_in.astype(jnp.float32)
    normed = norm_gain(tokens_float, first_gain).astype(jnp.bfloat16)
    raw = jnp.dot(normed, full_qkv, preferred_element_type=jnp.float32)
    query_raw = raw[:, :qc].reshape(group_rows, -1, HD)
    keys_raw = raw[:, qc : qc + kc].reshape(group_rows, -1, HD)
    values_low = raw[:, qc + kc :].astype(jnp.bfloat16).reshape(group_rows, -1, HD)
    kv_local = keys_raw.shape[1]
    grouping = query_raw.shape[1] // kv_local
    cosine, sine = rope_tables(positions)
    query_low = head_prep(query_raw, query_gain, cosine, sine).astype(jnp.bfloat16)
    keys_low = head_prep(keys_raw, key_gain, cosine, sine).astype(jnp.bfloat16)
    query_seq = query_low.reshape(count, length, kv_local, grouping, HD)
    keys_seq = keys_low.reshape(count, length, kv_local, HD)
    values_seq = values_low.reshape(count, length, kv_local, HD)
    mixed, log_total = lax.map(attend_forward, (query_seq, keys_seq, values_seq, prefix_len))
    mixed_low = mixed.reshape(group_rows, -1).astype(jnp.bfloat16)
    attn_part = jnp.einsum("th,dh->td", mixed_low, full_out, preferred_element_type=jnp.float32)
    middle = own_float + rs(attn_part.astype(jnp.bfloat16), parts, cid=2)
    grad_held, unused_tokens = lax.optimization_barrier((grad_out, tokens_all))
    grad_all = lax.all_gather(grad_held, "tp", axis=0, tiled=True)
    grad_middle, grad_second, ffn_part, grad_w_ffn = ffn(
        middle, second_gain[None], grad_all, ffn_set, parts, cid=3
    )

    def spread(value):
        return lax.psum_scatter(value, "fsdp", scatter_dimension=0, tiled=True)

    ffn_own = spread(grad_w_ffn)
    cos_all = jnp.concatenate([cosine[:, 0], cosine[:, 0]], axis=1)
    sin_all = jnp.concatenate([-sine[:, 0], sine[:, 0]], axis=1)
    heads = query_raw.shape[1]
    qkv_low = jnp.concatenate(
        [query_low.reshape(group_rows, -1), keys_low.reshape(group_rows, -1), values_low.reshape(group_rows, -1)],
        axis=1,
    )
    log_rows = jnp.pad(log_total.reshape(heads, group_rows), ((0, 8 - heads), (0, 0)))
    gain_rows = jnp.pad(jnp.stack([query_gain, key_gain]), ((0, 6), (0, 0)))
    out, grad_normed, grad_small, grad_w_attn = attn_back(
        grad_middle, middle, cos_all, sin_all, log_rows, gain_rows, prefix_len, attn_set,
        normed, qkv_low, raw[:, : qc + kc], mixed_low, ffn_part, parts, heads, kv_local, cid=5,
    )
    grad_w_attn, ffn_own = lax.optimization_barrier((grad_w_attn, ffn_own))
    attn_own = spread(grad_w_attn).astype(jnp.float32)
    ffn_own = ffn_own.astype(jnp.float32)
    grad_in, sums = final(
        grad_normed, hidden_in, grad_middle, first_gain[None], grad_second, grad_small, parts, groups, cid=6
    )
    place = lax.axis_index("fsdp") * head_slot
    return (
        out,
        grad_in,
        sums[0, :slot],
        attn_own[:, :qc],
        attn_own[:, qc : qc + kc],
        attn_own[:, qc + kc : qc + 2 * kc],
        attn_own[:, qc + 2 * kc :].T,
        lax.dynamic_slice_in_dim(sums[0, 2 * slot : 2 * slot + HD], place, head_slot),
        lax.dynamic_slice_in_dim(sums[0, 2 * slot + HD :], place, head_slot),
        sums[0, slot : 2 * slot],
        ffn_own[:, :fc],
        ffn_own[:, fc : 2 * fc],
        ffn_own[:, 2 * fc :].T,
    )


def solution(mesh):
    in_specs = (
        P(("fsdp", "tp"), None),
        P(("fsdp", "tp"), None),
        P("fsdp"),
        P("fsdp"),
        P("fsdp"),
        P("fsdp", "tp"),
        P("fsdp", "tp"),
        P("fsdp", "tp"),
        P("tp", "fsdp"),
        P("fsdp"),
        P("fsdp"),
        P("fsdp"),
        P("fsdp", "tp"),
        P("fsdp", "tp"),
        P("tp", "fsdp"),
    )
    out_specs = (
        P(("fsdp", "tp"), None),
        P(("fsdp", "tp"), None),
        P("fsdp"),
        P("fsdp", "tp"),
        P("fsdp", "tp"),
        P("fsdp", "tp"),
        P("tp", "fsdp"),
        P("fsdp"),
        P("fsdp"),
        P("fsdp"),
        P("fsdp", "tp"),
        P("fsdp", "tp"),
        P("tp", "fsdp"),
    )
    return jax.shard_map(
        per_device, mesh=mesh, in_specs=in_specs, out_specs=out_specs, check_vma=False
    )
```

```python
import functools
import math

import jax
import jax.numpy as jnp
from jax import lax
from jax.experimental import pallas as pl
from jax.experimental.pallas import tpu as pltpu
from jax.sharding import PartitionSpec as P

MESH = pl.DeviceIdType.MESH
VMEM_LIMIT = 67043328

HD = 128


EPS = 1e-06
ROPE_BASE = 1000000.0


def rope_tables(places):
    half = HD // 2
    ladder = jnp.arange(half, dtype=jnp.float32) * (2.0 / HD)
    frequency = jnp.exp(-ladder * math.log(ROPE_BASE))
    angle = places.astype(jnp.float32)[:, None] * frequency[None, :]
    cosine, sine = jnp.cos(angle), jnp.sin(angle)
    return jnp.concatenate([cosine, cosine], axis=1), jnp.concatenate([-sine, sine], axis=1)


def greet(me, n, axis):
    barrier = pltpu.get_barrier_semaphore()
    for d in (1, -1):
        @pl.when((me + d >= 0) & (me + d < n))
        def _():
            pl.semaphore_signal(barrier, inc=1, device_id={axis: me + d}, device_id_type=MESH)
    edge = (me == 0) | (me == n - 1)

    @pl.when(edge)
    def _():
        pl.semaphore_wait(barrier, 1)

    @pl.when(~edge)
    def _():
        pl.semaphore_wait(barrier, 2)

def inside(v, n):
    return (v >= 0) & (v < n)

def exchange_plan(n, me):
    return ((0, 1, me), (1, -1, n - 1 - me))


def dot_t(left, right):
    return lax.dot_general(left, right, (((1,), (1,)), ((), ())), preferred_element_type=jnp.float32)


def entry_kernel(
    n, groups, head_slot, x_ref, pack_ref, normed_ref, gattn_ref, gffn_ref, small_ref,
    tokens, grecv, send_sem, recv_sem, gs_sem, gr_sem,
):
    me = lax.axis_index("tp")
    mine = lax.axis_index("fsdp")
    rows_own, width = x_ref.shape
    slot = width // groups
    barrier = pltpu.get_barrier_semaphore()
    for f in range(groups):
        @pl.when(mine != f)
        def _():
            pl.semaphore_signal(barrier, inc=1, device_id={"fsdp": f}, device_id_type=MESH)
    for d in (1, -1):
        @pl.when(inside(me + d, n))
        def _():
            pl.semaphore_signal(barrier, inc=1, device_id={"tp": me + d}, device_id_type=MESH)
    edge = (me == 0) | (me == n - 1)

    @pl.when(edge)
    def _():
        pl.semaphore_wait(barrier, groups)

    @pl.when(~edge)
    def _():
        pl.semaphore_wait(barrier, groups + 1)

    def block(j):
        return pl.ds(pl.multiple_of(j * rows_own, rows_own), rows_own)

    def passing(di, d, k, sender):
        j = sender - d * k
        src = x_ref if k == 0 else tokens.at[block(j)]
        return pltpu.make_async_remote_copy(
            src_ref=src, dst_ref=tokens.at[block(j)], send_sem=send_sem.at[di, k], recv_sem=recv_sem.at[di, k],
            device_id={"tp": sender + d}, device_id_type=MESH,
        )

    def to_peer(f, sender):
        return pltpu.make_async_remote_copy(
            src_ref=pack_ref, dst_ref=grecv.at[sender], send_sem=gs_sem.at[f], recv_sem=gr_sem.at[sender],
            device_id={"fsdp": f}, device_id_type=MESH,
        )

    sides = ((0, 1), (1, -1))
    for di, d in sides:
        @pl.when(inside(me + d, n))
        def _():
            passing(di, d, 0, me).start()
    for f in range(groups):
        @pl.when(mine != f)
        def _():
            to_peer(f, mine).start()
    grecv[mine] = pack_ref[...]
    for f in range(groups):
        @pl.when(mine != f)
        def _():
            to_peer(f, f).wait_recv()
    small_ref[...] = jnp.zeros_like(small_ref)
    for f in range(groups):
        at = slice(f * slot, (f + 1) * slot)
        gattn_ref[:, at] = grecv[f, :, :slot]
        gffn_ref[:, at] = grecv[f, :, slot : 2 * slot]
        for row in range(2):
            part = grecv[f, :, 2 * slot + row * HD : 2 * slot + (row + 1) * HD]
            small_ref[row : row + 1, :] += part if f == 0 else pltpu.roll(part, f * head_slot, 1)

    def normalize(source, at):
        value = source.astype(jnp.float32)
        inverse = lax.rsqrt(jnp.mean(value * value, axis=-1, keepdims=True) + EPS)
        normed_ref[at, :] = (value * inverse * gattn_ref[...]).astype(jnp.bfloat16)

    normalize(x_ref[...], block(me))
    for k in range(1, n):
        for di, d in sides:
            @pl.when(inside(me - d * k, n))
            def _():
                passing(di, d, k - 1, me - d).wait_recv()
            if k < n - 1:
                @pl.when(inside(me - d * k, n) & inside(me + d, n))
                def _():
                    passing(di, d, k, me).start()
        for di, d in sides:
            @pl.when(inside(me - d * k, n))
            def _():
                normalize(tokens[block(me - d * k), :], block(me - d * k))
    for k in range(n - 1):
        for di, d in sides:
            @pl.when(inside(me - d * k, n) & inside(me + d, n))
            def _():
                passing(di, d, k, me).wait_send()
    for f in range(groups):
        @pl.when(mine != f)
        def _():
            to_peer(f, mine).wait_send()


def entry(x, pack, n, groups, head_slot, cid):
    rows_own, width = x.shape
    vmem = pl.BlockSpec(memory_space=pltpu.VMEM)
    dma = pltpu.SemaphoreType.DMA
    return pl.pallas_call(
        functools.partial(entry_kernel, n, groups, head_slot),
        out_shape=(
            jax.ShapeDtypeStruct((rows_own * n, width), jnp.bfloat16),
            jax.ShapeDtypeStruct((1, width), jnp.float32),
            jax.ShapeDtypeStruct((1, width), jnp.float32),
            jax.ShapeDtypeStruct((8, HD), jnp.float32),
        ),
        in_specs=[vmem] * 2,
        out_specs=(vmem,) * 4,
        scratch_shapes=[
            pltpu.VMEM((rows_own * n, width), jnp.bfloat16),
            pltpu.VMEM((groups,) + pack.shape, jnp.float32),
            dma((2, n - 1)), dma((2, n - 1)), dma((groups,)), dma((groups,)),
        ],
        compiler_params=pltpu.CompilerParams(
            collective_id=cid, has_side_effects=True, vmem_limit_bytes=32 << 20
        ),
        cost_estimate=pl.CostEstimate(flops=1 << 34, bytes_accessed=200 << 20, transcendentals=0),
        name="entry",
    )(x, pack)


def attn_kernel(
    n, axis, heads, kv_heads,
    x_ref, go_ref, normed_ref, cos_ref, sin_ref, gain_ref, prefix_ref, w_hbm,
    mid_ref, go_all, qkv, raw, mixed, lse_ref,
    wbuf, part, values_t, rb, load_sem, send_ag, recv_ag, send_rs, recv_rs,
):
    me = lax.axis_index(axis)
    rows_own, width = x_ref.shape
    total = rows_own * n
    qc, kc = heads * HD, kv_heads * HD
    group = heads // kv_heads
    scale = 1.0 / math.sqrt(HD)
    load = pltpu.make_async_copy(w_hbm, wbuf, load_sem.at[0])
    load.start()
    greet(me, n, axis)

    def block(j):
        return pl.ds(pl.multiple_of(j * rows_own, rows_own), rows_own)

    def passing(di, d, k, sender):
        j = sender - d * k
        src = go_ref if k == 0 else go_all.at[block(j)]
        return pltpu.make_async_remote_copy(
            src_ref=src, dst_ref=go_all.at[block(j)], send_sem=send_ag.at[di, k], recv_sem=recv_ag.at[di, k],
            device_id={axis: sender + d}, device_id_type=MESH,
        )

    def owner(d, q):
        return n - 1 - q if d > 0 else q

    def item(di, d, q, sender, first):
        src = part.at[block(owner(d, q))] if first else rb.at[di, q]
        return pltpu.make_async_remote_copy(
            src_ref=src, dst_ref=rb.at[di, q], send_sem=send_rs.at[di, q], recv_sem=recv_rs.at[di, q],
            device_id={axis: sender + d}, device_id_type=MESH,
        )

    sides = ((0, 1), (1, -1))
    ways = exchange_plan(n, me)

    def gather_step(k):
        for di, d in sides:
            if k > 0:
                @pl.when(inside(me - d * k, n))
                def _():
                    passing(di, d, k - 1, me - d).wait_recv()
            if k < n - 1:
                @pl.when(inside(me - d * k, n) & inside(me + d, n))
                def _():
                    passing(di, d, k, me).start()

    def sums_step(t):
        for di, d, dist in ways:
            @pl.when((dist > 0) & (t >= dist))
            def _():
                q = t - dist
                item(di, d, q, me - d, False).wait_recv()
                rb[di, q] = (rb[di, q].astype(jnp.float32) + part[block(owner(d, q)), :].astype(jnp.float32)).astype(rb.dtype)
                item(di, d, q, me, False).start()

    gather_step(0)
    go_all[block(me), :] = go_ref[...]
    lse_ref[...] = jnp.zeros_like(lse_ref)
    load.wait()

    def project(j, carry):
        at = block(j)
        value = jnp.dot(normed_ref[at, :], wbuf[:, : qc + 2 * kc], preferred_element_type=jnp.float32)
        raw[at, :] = value[:, : qc + kc]
        for h in range(heads + kv_heads):
            head = value[:, h * HD : (h + 1) * HD]
            gain = gain_ref[0:1, :] if h < heads else gain_ref[1:2, :]
            scaled = head * lax.rsqrt(jnp.mean(head * head, axis=-1, keepdims=True) + EPS) * gain
            turned = scaled * cos_ref[at, :] + pltpu.roll(scaled, HD // 2, 1) * sin_ref[at, :]
            qkv[at, h * HD : (h + 1) * HD] = turned.astype(jnp.bfloat16)
        qkv[at, qc + kc :] = value[:, qc + kc :].astype(jnp.bfloat16)
        return carry

    lax.fori_loop(0, n, project, 0)
    for g in range(kv_heads):
        values_t[g] = qkv[:, qc + kc + g * HD : qc + kc + (g + 1) * HD].T
    prefix = prefix_ref[0]

    def attend(i, carry):
        @pl.when(i == 2)
        def _():
            gather_step(1)
        j = jnp.where(2 * me < n, n - 1 - i, i)
        at = block(j)
        key_at = lax.broadcasted_iota(jnp.int32, (total, rows_own), 0)
        query_at = lax.broadcasted_iota(jnp.int32, (total, rows_own), 1) + j * rows_own
        seen = (key_at <= query_at) | (key_at < prefix)
        for h in range(heads):
            g = h // group
            ks, hs = qc + g * HD, h * HD
            scores = jnp.where(seen, dot_t(qkv[:, ks : ks + HD], qkv[at, hs : hs + HD]) * scale, -1e30)
            peak = jnp.max(scores, axis=0, keepdims=True)
            raised = jnp.exp(scores - peak)
            weight = jnp.sum(raised, axis=0, keepdims=True)
            lse_ref[h : h + 1, at] = peak + jnp.log(weight)
            shares = (raised * (1.0 / weight)).astype(jnp.bfloat16)
            mixed[at, hs : hs + HD] = jnp.dot(values_t[g], shares, preferred_element_type=jnp.float32).T.astype(jnp.bfloat16)
        cut = width // 4
        for f in range(4):
            cols = pl.ds(f * cut, cut)
            part[at, cols] = dot_t(mixed[at, :], wbuf[cols, qc + 2 * kc :]).astype(jnp.bfloat16)
        for di, d, dist in ways:
            @pl.when((dist == 0) & (i < n - 1))
            def _():
                item(di, d, i, me, True).start()
        return carry

    lax.fori_loop(0, n, attend, 0)
    for t in range(1, n):
        if t < n - 1:
            sums_step(t)
        if t + 1 < n:
            gather_step(t + 1)
    for di, d, dist in ways:
        @pl.when(dist > 0)
        def _():
            item(di, d, n - 1 - dist, me - d, False).wait_recv()
    own = x_ref[...].astype(jnp.float32) + part[block(me), :].astype(jnp.float32)
    @pl.when(me == 0)
    def _():
        mid_ref[...] = own + rb[1, 0].astype(jnp.float32)
    @pl.when(me == n - 1)
    def _():
        mid_ref[...] = own + rb[0, 0].astype(jnp.float32)
    @pl.when((me > 0) & (me < n - 1))
    def _():
        mid_ref[...] = own + rb[0, n - 1 - me].astype(jnp.float32) + rb[1, me].astype(jnp.float32)
    for k in range(n - 1):
        for di, d in sides:
            @pl.when(inside(me - d * k, n) & inside(me + d, n))
            def _():
                passing(di, d, k, me).wait_send()
    for t in range(n - 1):
        for di, d, dist in ways:
            @pl.when(t >= dist)
            def _():
                item(di, d, t - dist, me, False).wait_send()


def attn(x, go, normed, cos2, sin2, gains, prefix, w, n, heads, kv_heads, cid, axis="tp"):
    rows_own, width = x.shape
    total = rows_own * n
    vmem = pl.BlockSpec(memory_space=pltpu.VMEM)
    any_space = pl.BlockSpec(memory_space=pl.ANY)
    dma = pltpu.SemaphoreType.DMA
    cols = (heads + 2 * kv_heads) * HD
    return pl.pallas_call(
        functools.partial(attn_kernel, n, axis, heads, kv_heads),
        out_shape=(
            jax.ShapeDtypeStruct((rows_own, width), jnp.float32),
            jax.ShapeDtypeStruct((total, width), jnp.bfloat16),
            jax.ShapeDtypeStruct((total, cols), jnp.bfloat16),
            jax.ShapeDtypeStruct((total, cols - kv_heads * HD), jnp.float32),
            jax.ShapeDtypeStruct((total, heads * HD), jnp.bfloat16),
            jax.ShapeDtypeStruct((8, total), jnp.float32),
        ),
        in_specs=[vmem] * 6 + [pl.BlockSpec(memory_space=pltpu.SMEM), any_space],
        out_specs=(vmem,) * 6,
        scratch_shapes=[
            pltpu.VMEM(w.shape, jnp.bfloat16),
            pltpu.VMEM((total, width), jnp.bfloat16),
            pltpu.VMEM((kv_heads, HD, total), jnp.bfloat16),
            pltpu.VMEM((2, n - 1, rows_own, width), jnp.bfloat16),
            dma((1,)), dma((2, n - 1)), dma((2, n - 1)), dma((2, n - 1)), dma((2, n - 1)),
        ],
        compiler_params=pltpu.CompilerParams(
            collective_id=cid, has_side_effects=True, vmem_limit_bytes=VMEM_LIMIT
        ),
        cost_estimate=pl.CostEstimate(flops=1 << 34, bytes_accessed=300 << 20, transcendentals=0),
        name="attn",
    )(x, go, normed, cos2, sin2, gains, prefix, w)


def ffn_kernel(
    n, axis, mid_ref, gain_ref, go_ref, w_ref, gmid_ref, gffn_ref, part_ref, gw_ref,
    branch, wbuf, act, gpart, rb, w_sem, out_sem, send_ag, recv_ag, send_rs, recv_rs,
):
    me = lax.axis_index(axis)
    rows_own, width = mid_ref.shape
    hidden = wbuf.shape[2]
    cut = hidden // 3
    wcut = width // 4
    loads = [
        pltpu.make_async_copy(w_ref.at[:, pl.ds(m * hidden, hidden)], wbuf.at[m], w_sem.at[m])
        for m in range(3)
    ]
    for load in loads:
        load.start()

    def block(j):
        return pl.ds(pl.multiple_of(j * rows_own, rows_own), rows_own)

    mid = mid_ref[...]
    inverse = lax.rsqrt(jnp.mean(mid * mid, axis=-1, keepdims=True) + EPS)
    branch[block(me), :] = (mid * inverse * gain_ref[...]).astype(jnp.bfloat16)
    greet(me, n, axis)

    def passing(di, d, k, sender):
        j = sender - d * k
        return pltpu.make_async_remote_copy(
            src_ref=branch.at[block(j)], dst_ref=branch.at[block(j)],
            send_sem=send_ag.at[di, k], recv_sem=recv_ag.at[di, k],
            device_id={axis: sender + d}, device_id_type=MESH,
        )

    sides = ((0, 1), (1, -1))
    for di, d in sides:
        @pl.when(inside(me + d, n))
        def _():
            passing(di, d, 0, me).start()
    for load in loads:
        load.wait()

    def chunk(j):
        at = block(j)
        for f in range(3):
            cols = pl.ds(f * cut, cut)
            gate = jnp.dot(branch[at, :], wbuf[0, :, cols], preferred_element_type=jnp.float32)
            upward = jnp.dot(branch[at, :], wbuf[1, :, cols], preferred_element_type=jnp.float32)
            sig = jax.nn.sigmoid(gate)
            silu = gate * sig
            act[2, at, cols] = (silu * upward).astype(jnp.bfloat16)
            gprod = jnp.dot(go_ref[at, :], wbuf[2, :, cols], preferred_element_type=jnp.float32)
            act[0, at, cols] = (gprod * upward * (sig * (1.0 + gate * (1.0 - sig)))).astype(jnp.bfloat16)
            act[1, at, cols] = (gprod * silu).astype(jnp.bfloat16)
        for f in range(4):
            cols = pl.ds(f * wcut, wcut)
            part_ref[at, cols] = dot_t(act[2, at, :], wbuf[2, cols, :]).astype(jnp.bfloat16)
            gpart[at, cols] = (
                dot_t(act[0, at, :], wbuf[0, cols, :]) + dot_t(act[1, at, :], wbuf[1, cols, :])
            ).astype(jnp.bfloat16)

    def distance(k, carry):
        for di, d in sides:
            @pl.when((k > 0) & inside(me - d * k, n))
            def _():
                passing(di, d, k - 1, me - d).wait_recv()
                @pl.when(inside(me + d, n))
                def _():
                    passing(di, d, k, me).start()
        low = inside(me - k, n)
        high = (k > 0) & inside(me + k, n)
        number = low.astype(jnp.int32) + high.astype(jnp.int32)

        def one(i, c):
            j = jnp.where((i == 0) & low, me - k, me + k)
            chunk(j)
            return c

        lax.fori_loop(0, number, one, 0)
        return carry

    lax.fori_loop(0, n, distance, 0)

    def owner(d, q):
        return n - 1 - q if d > 0 else q

    def item(di, d, q, sender, first):
        src = gpart.at[block(owner(d, q))] if first else rb.at[di, q]
        return pltpu.make_async_remote_copy(
            src_ref=src, dst_ref=rb.at[di, q], send_sem=send_rs.at[di, q], recv_sem=recv_rs.at[di, q],
            device_id={axis: sender + d}, device_id_type=MESH,
        )

    ways = ((0, 1, me), (1, -1, n - 1 - me))
    for q in range(n - 1):
        for di, d, dist in ways:
            @pl.when(dist == 0)
            def _():
                item(di, d, q, me, True).start()

    tile = width // 4

    def leave(m, r):
        return pltpu.make_async_copy(
            wbuf.at[m, pl.ds(pl.multiple_of(r * tile, tile), tile)],
            gw_ref.at[pl.ds(pl.multiple_of(r * tile, tile), tile), pl.ds(m * hidden, hidden)],
            out_sem.at[m, r],
        )

    def weights(m, left):
        def one(r, c):
            at = pl.ds(pl.multiple_of(r * tile, tile), tile)
            wbuf[m, at, :] = lax.dot_general(
                left[:, at], act[m], (((0,), (0,)), ((), ())), preferred_element_type=jnp.float32
            ).astype(jnp.bfloat16)
            leave(m, r).start()
            return c

        lax.fori_loop(0, 4, one, 0)

    todo = [(2, go_ref), (0, branch), (1, branch)]
    for t in range(1, n):
        if todo:
            weights(*todo.pop(0))
        if t == n - 1:
            while todo:
                weights(*todo.pop(0))
            break
        for di, d, dist in ways:
            @pl.when((dist > 0) & (t >= dist))
            def _():
                q = t - dist
                item(di, d, q, me - d, False).wait_recv()
                rb[di, q] = (rb[di, q].astype(jnp.float32) + gpart[block(owner(d, q)), :].astype(jnp.float32)).astype(rb.dtype)
                item(di, d, q, me, False).start()
    for di, d, dist in ways:
        @pl.when(dist > 0)
        def _():
            item(di, d, n - 1 - dist, me - d, False).wait_recv()
    @pl.when(me == 0)
    def _():
        gmid_ref[...] = gpart[block(0), :].astype(jnp.float32) + rb[1, 0].astype(jnp.float32)
    @pl.when(me == n - 1)
    def _():
        gmid_ref[...] = gpart[block(n - 1), :].astype(jnp.float32) + rb[0, 0].astype(jnp.float32)
    @pl.when((me > 0) & (me < n - 1))
    def _():
        gmid_ref[...] = gpart[block(me), :].astype(jnp.float32) + rb[0, n - 1 - me].astype(jnp.float32) + rb[1, me].astype(jnp.float32)
    mid = mid_ref[...]
    inverse = lax.rsqrt(jnp.mean(mid * mid, axis=-1, keepdims=True) + EPS)
    unit = mid * inverse
    grad = gmid_ref[...]
    gffn_ref[...] = jnp.sum(grad * unit, axis=0, keepdims=True)
    scaled = grad * gain_ref[...]
    gmid_ref[...] = go_ref[block(me), :].astype(jnp.float32) + inverse * (scaled - unit * jnp.mean(scaled * unit, axis=-1, keepdims=True))

    for k in range(n - 1):
        for di, d in sides:
            @pl.when(inside(me - d * k, n) & inside(me + d, n))
            def _():
                passing(di, d, k, me).wait_send()
    for t in range(n - 1):
        for di, d, dist in ways:
            @pl.when(t >= dist)
            def _():
                item(di, d, t - dist, me, False).wait_send()
    for m in range(3):
        for r in range(4):
            leave(m, r).wait()


def ffn(mid, gain, go, w, n, cid, axis="tp"):
    rows_own, width = mid.shape
    total = rows_own * n
    hidden = w.shape[1] // 3
    vmem = pl.BlockSpec(memory_space=pltpu.VMEM)
    any_space = pl.BlockSpec(memory_space=pl.ANY)
    dma = pltpu.SemaphoreType.DMA
    return pl.pallas_call(
        functools.partial(ffn_kernel, n, axis),
        out_shape=(
            jax.ShapeDtypeStruct((rows_own, width), jnp.float32),
            jax.ShapeDtypeStruct((1, width), jnp.float32),
            jax.ShapeDtypeStruct((total, width), jnp.bfloat16),
            jax.ShapeDtypeStruct(w.shape, jnp.bfloat16),
        ),
        in_specs=[vmem, vmem, vmem, any_space],
        out_specs=(vmem, vmem, vmem, any_space),
        scratch_shapes=[
            pltpu.VMEM((total, width), jnp.bfloat16),
            pltpu.VMEM((3, width, hidden), jnp.bfloat16),
            pltpu.VMEM((3, total, hidden), jnp.bfloat16),
            pltpu.VMEM((total, width), jnp.bfloat16),
            pltpu.VMEM((2, n - 1, rows_own, width), jnp.bfloat16),
            dma((3,)), dma((3, 4)), dma((2, n - 1)), dma((2, n - 1)), dma((2, n - 1)), dma((2, n - 1)),
        ],
        compiler_params=pltpu.CompilerParams(
            collective_id=cid, has_side_effects=True, vmem_limit_bytes=VMEM_LIMIT
        ),
        cost_estimate=pl.CostEstimate(
            flops=18 * total * width * hidden, bytes_accessed=12 * width * hidden, transcendentals=0
        ),
        name="ffn",
    )(mid, gain, go, w)


def unroll_rot(value, cos2, sin2):
    return value * cos2 - pltpu.roll(value, HD // 2, 1) * sin2


def attn_back_kernel(
    n, axis, heads, kv_heads,
    gmid_ref, mid_ref, cos_ref, sin_ref, lse_ref, gain_ref, prefix_ref,
    w_hbm, normed_hbm, qkv_hbm, raw_hbm, mixed_hbm, part_hbm,
    out_ref, gn_ref, gsum_ref, gw_ref,
    wbuf, normed, qkv, raw, mixed, part, gm, gmix, keys_t, dk, dv, gqkv, rb,
    load_sem, out_sem, send_ag, recv_ag, send_rs, recv_rs,
):
    me = lax.axis_index(axis)
    rows_own, width = gmid_ref.shape
    total = rows_own * n
    qc, kc = heads * HD, kv_heads * HD
    group = heads // kv_heads
    scale = 1.0 / math.sqrt(HD)
    pairs = ((w_hbm, wbuf), (qkv_hbm, qkv), (raw_hbm, raw), (part_hbm, part), (normed_hbm, normed), (mixed_hbm, mixed))
    loads = [pltpu.make_async_copy(src, dst, load_sem.at[i]) for i, (src, dst) in enumerate(pairs)]
    for load in loads:
        load.start()

    def block(j):
        return pl.ds(pl.multiple_of(j * rows_own, rows_own), rows_own)

    gm[block(me), :] = gmid_ref[...].astype(jnp.bfloat16)
    dk[...] = jnp.zeros_like(dk)
    dv[...] = jnp.zeros_like(dv)
    gsum_ref[...] = jnp.zeros_like(gsum_ref)
    greet(me, n, axis)

    def passing(di, d, k, sender):
        j = sender - d * k
        return pltpu.make_async_remote_copy(
            src_ref=gm.at[block(j)], dst_ref=gm.at[block(j)],
            send_sem=send_ag.at[di, k], recv_sem=recv_ag.at[di, k],
            device_id={axis: sender + d}, device_id_type=MESH,
        )

    def owner(d, q):
        return n - 1 - q if d > 0 else q

    def item(di, d, q, sender, first):
        src = part.at[block(owner(d, q))] if first else rb.at[di, q]
        return pltpu.make_async_remote_copy(
            src_ref=src, dst_ref=rb.at[di, q], send_sem=send_rs.at[di, q], recv_sem=recv_rs.at[di, q],
            device_id={axis: sender + d}, device_id_type=MESH,
        )

    sides = ((0, 1), (1, -1))
    ways = exchange_plan(n, me)
    for di, d in sides:
        @pl.when(inside(me + d, n))
        def _():
            passing(di, d, 0, me).start()
    for load in loads[:3]:
        load.wait()
    for g in range(kv_heads):
        keys_t[g] = qkv[:, qc + g * HD : qc + (g + 1) * HD].T
    loads[3].wait()
    prefix = prefix_ref[0]

    def unit_of(at, first):
        value = raw[at, first : first + HD]
        inverse = lax.rsqrt(jnp.mean(value * value, axis=-1, keepdims=True) + EPS)
        return value * inverse, inverse

    def normed_back(grad, at, first, gain, place):
        unit, inverse = unit_of(at, first)
        turned = unroll_rot(grad, cos_ref[at, :], sin_ref[at, :])
        gsum_ref[place : place + 1, :] += jnp.sum(turned * unit, axis=0, keepdims=True)
        scaled = turned * gain
        return (inverse * (scaled - unit * jnp.mean(scaled * unit, axis=-1, keepdims=True))).astype(jnp.bfloat16)

    def chunk(j):
        at = block(j)
        gmix[...] = jnp.dot(gm[at, :], wbuf[:, qc + 2 * kc :], preferred_element_type=jnp.float32).astype(jnp.bfloat16)
        key_at = lax.broadcasted_iota(jnp.int32, (total, rows_own), 0)
        query_at = lax.broadcasted_iota(jnp.int32, (total, rows_own), 1) + j * rows_own
        seen = (key_at <= query_at) | (key_at < prefix)
        for h in range(heads):
            g = h // group
            ks, vs, hs = qc + g * HD, qc + kc + g * HD, h * HD
            q = qkv[at, hs : hs + HD]
            gx = gmix[:, hs : hs + HD]
            scores = dot_t(qkv[:, ks : ks + HD], q) * scale
            shares = jnp.where(seen, jnp.exp(scores - lse_ref[h : h + 1, at]), 0.0)
            grad_shares = dot_t(qkv[:, vs : vs + HD], gx)
            delta = jnp.sum(grad_shares * shares, axis=0, keepdims=True)
            low = (shares * (grad_shares - delta) * scale).astype(jnp.bfloat16)
            gcols = pl.ds(g * HD, HD)
            dk[:, gcols] += jnp.dot(low, q, preferred_element_type=jnp.float32)
            dv[:, gcols] += jnp.dot(shares.astype(jnp.bfloat16), gx, preferred_element_type=jnp.float32)
            dq = jnp.dot(keys_t[g], low, preferred_element_type=jnp.float32).T
            gqkv[at, hs : hs + HD] = normed_back(dq, at, hs, gain_ref[0:1, :], 0)

    def sums_step(t):
        for di, d, dist in ways:
            @pl.when((dist > 0) & (t >= dist))
            def _():
                q = t - dist
                item(di, d, q, me - d, False).wait_recv()
                rb[di, q] = (rb[di, q].astype(jnp.float32) + part[block(owner(d, q)), :].astype(jnp.float32)).astype(rb.dtype)
                item(di, d, q, me, False).start()

    def distance(k, carry):
        for di, d in sides:
            @pl.when((k > 0) & inside(me - d * k, n))
            def _():
                passing(di, d, k - 1, me - d).wait_recv()
                @pl.when(inside(me + d, n))
                def _():
                    passing(di, d, k, me).start()

        for di, d, dist in ways:
            @pl.when((k == 1) & (dist == 0))
            def _():
                for q in range(n - 1):
                    item(di, d, q, me, True).start()

        @pl.when(k > 1)
        def _():
            sums_step(k - 1)

        low = inside(me - k, n)
        high = (k > 0) & inside(me + k, n)
        number = low.astype(jnp.int32) + high.astype(jnp.int32)

        def one(i, c):
            chunk(jnp.where((i == 0) & low, me - k, me + k))
            return c

        lax.fori_loop(0, number, one, 0)
        return carry

    lax.fori_loop(0, n, distance, 0)

    for load in loads[4:]:
        load.wait()

    def finish(j, carry):
        at = block(j)
        for g in range(kv_heads):
            ks, vs = qc + g * HD, qc + kc + g * HD
            gqkv[at, ks : ks + HD] = normed_back(dk[at, g * HD : (g + 1) * HD], at, ks, gain_ref[1:2, :], 1)
            gqkv[at, vs : vs + HD] = dv[at, g * HD : (g + 1) * HD].astype(jnp.bfloat16)
        cut = width // 4
        for f in range(4):
            cols = pl.ds(f * cut, cut)
            gn_ref[at, cols] = dot_t(gqkv[at, :], wbuf[cols, : qc + 2 * kc]).astype(jnp.bfloat16)
        return carry

    lax.fori_loop(0, n, finish, 0)

    tile = width // 4

    def leave(r):
        at = pl.ds(pl.multiple_of(r * tile, tile), tile)
        return pltpu.make_async_copy(wbuf.at[at], gw_ref.at[at], out_sem.at[r])

    def weights(r, carry):
        at = pl.ds(pl.multiple_of(r * tile, tile), tile)
        wbuf[at, : qc + 2 * kc] = lax.dot_general(
            normed[:, at], gqkv[...], (((0,), (0,)), ((), ())), preferred_element_type=jnp.float32
        ).astype(jnp.bfloat16)
        wbuf[at, qc + 2 * kc :] = lax.dot_general(
            gm[:, at], mixed[...], (((0,), (0,)), ((), ())), preferred_element_type=jnp.float32
        ).astype(jnp.bfloat16)
        leave(r).start()
        return carry

    lax.fori_loop(0, 4, weights, 0)

    for di, d, dist in ways:
        @pl.when(dist > 0)
        def _():
            item(di, d, n - 1 - dist, me - d, False).wait_recv()
    own = mid_ref[...] + part[block(me), :].astype(jnp.float32)
    @pl.when(me == 0)
    def _():
        out_ref[...] = (own + rb[1, 0].astype(jnp.float32)).astype(out_ref.dtype)
    @pl.when(me == n - 1)
    def _():
        out_ref[...] = (own + rb[0, 0].astype(jnp.float32)).astype(out_ref.dtype)
    @pl.when((me > 0) & (me < n - 1))
    def _():
        out_ref[...] = (own + rb[0, n - 1 - me].astype(jnp.float32) + rb[1, me].astype(jnp.float32)).astype(out_ref.dtype)

    for k in range(n - 1):
        for di, d in sides:
            @pl.when(inside(me - d * k, n) & inside(me + d, n))
            def _():
                passing(di, d, k, me).wait_send()
    for t in range(n - 1):
        for di, d, dist in ways:
            @pl.when(t >= dist)
            def _():
                item(di, d, t - dist, me, False).wait_send()
    for r in range(4):
        leave(r).wait()


def attn_back(gmid, mid, cos2, sin2, lse, gains, prefix, w, normed, qkv, raw, mixed, part, n, heads, kv_heads, cid, axis="tp"):
    rows_own, width = gmid.shape
    total = rows_own * n
    vmem = pl.BlockSpec(memory_space=pltpu.VMEM)
    any_space = pl.BlockSpec(memory_space=pl.ANY)
    dma = pltpu.SemaphoreType.DMA
    return pl.pallas_call(
        functools.partial(attn_back_kernel, n, axis, heads, kv_heads),
        out_shape=(
            jax.ShapeDtypeStruct((rows_own, width), jnp.bfloat16),
            jax.ShapeDtypeStruct((total, width), jnp.bfloat16),
            jax.ShapeDtypeStruct((8, HD), jnp.float32),
            jax.ShapeDtypeStruct(w.shape, jnp.bfloat16),
        ),
        in_specs=[vmem] * 6 + [pl.BlockSpec(memory_space=pltpu.SMEM)] + [any_space] * 6,
        out_specs=(vmem, vmem, vmem, any_space),
        scratch_shapes=[
            pltpu.VMEM(w.shape, jnp.bfloat16),
            pltpu.VMEM(normed.shape, jnp.bfloat16),
            pltpu.VMEM(qkv.shape, jnp.bfloat16),
            pltpu.VMEM(raw.shape, jnp.float32),
            pltpu.VMEM(mixed.shape, jnp.bfloat16),
            pltpu.VMEM(part.shape, jnp.bfloat16),
            pltpu.VMEM((total, width), jnp.bfloat16),
            pltpu.VMEM((rows_own, heads * HD), jnp.bfloat16),
            pltpu.VMEM((kv_heads, HD, total), jnp.bfloat16),
            pltpu.VMEM((total, kv_heads * HD), jnp.float32),
            pltpu.VMEM((total, kv_heads * HD), jnp.float32),
            pltpu.VMEM(qkv.shape, jnp.bfloat16),
            pltpu.VMEM((2, n - 1, rows_own, width), jnp.bfloat16),
            dma((6,)), dma((4,)), dma((2, n - 1)), dma((2, n - 1)), dma((2, n - 1)), dma((2, n - 1)),
        ],
        compiler_params=pltpu.CompilerParams(
            collective_id=cid, has_side_effects=True, vmem_limit_bytes=VMEM_LIMIT
        ),
        cost_estimate=pl.CostEstimate(flops=30 * total * width * HD, bytes_accessed=40 * total * width, transcendentals=0),
        name="attn_back",
    )(gmid, mid, cos2, sin2, lse, gains, prefix, w, normed, qkv, raw, mixed, part)


def final_kernel(
    n, groups, p_ref, x_ref, gmid_ref, gain_ref, gffn_ref, small_ref, dx_ref, total_ref,
    rb, gsend, grecv, tsend, trecv, send_sem, recv_sem, gs_sem, gr_sem, ts_sem, tr_sem,
):
    me = lax.axis_index("tp")
    mine = lax.axis_index("fsdp")
    rows_own, width = dx_ref.shape
    slot = width // groups
    barrier = pltpu.get_barrier_semaphore()
    for f in range(groups):
        @pl.when(mine != f)
        def _():
            pl.semaphore_signal(barrier, inc=1, device_id={"fsdp": f}, device_id_type=MESH)
    for p in range(n):
        @pl.when(me != p)
        def _():
            pl.semaphore_signal(barrier, inc=1, device_id={"tp": p}, device_id_type=MESH)
    pl.semaphore_wait(barrier, groups + n - 2)

    def block(j):
        return pl.ds(pl.multiple_of(j * rows_own, rows_own), rows_own)

    def owner(d, q):
        return n - 1 - q if d > 0 else q

    halves = 2
    half = rows_own // halves

    def item(di, d, q, s, sender, first):
        at = pl.ds(s * half, half)
        src = p_ref.at[pl.ds(pl.multiple_of(owner(d, q) * rows_own + s * half, half), half)] if first else rb.at[di, q, at]
        return pltpu.make_async_remote_copy(
            src_ref=src, dst_ref=rb.at[di, q, at], send_sem=send_sem.at[di, q, s], recv_sem=recv_sem.at[di, q, s],
            device_id={"tp": sender + d}, device_id_type=MESH,
        )

    ways = exchange_plan(n, me)
    for q in range(n - 1):
        for s in range(halves):
            for di, d, dist in ways:
                @pl.when(dist == 0)
                def _():
                    item(di, d, q, s, me, True).start()
    for t in range(1, n - 1):
        for s in range(halves):
            for di, d, dist in ways:
                @pl.when((dist > 0) & (t >= dist))
                def _():
                    q = t - dist
                    at = pl.ds(s * half, half)
                    item(di, d, q, s, me - d, False).wait_recv()
                    mine_at = pl.ds(pl.multiple_of(owner(d, q) * rows_own + s * half, half), half)
                    rb[di, q, at, :] = (rb[di, q, at, :].astype(jnp.float32) + p_ref[mine_at, :].astype(jnp.float32)).astype(rb.dtype)
                    item(di, d, q, s, me, False).start()
    for s in range(halves):
        for di, d, dist in ways:
            @pl.when(dist > 0)
            def _():
                item(di, d, n - 1 - dist, s, me - d, False).wait_recv()
    own = p_ref[block(me), :].astype(jnp.float32)
    @pl.when(me == 0)
    def _():
        dx_ref[...] = own + rb[1, 0].astype(jnp.float32)
    @pl.when(me == n - 1)
    def _():
        dx_ref[...] = own + rb[0, 0].astype(jnp.float32)
    @pl.when((me > 0) & (me < n - 1))
    def _():
        dx_ref[...] = own + rb[0, n - 1 - me].astype(jnp.float32) + rb[1, me].astype(jnp.float32)

    x = x_ref[...].astype(jnp.float32)
    inverse = lax.rsqrt(jnp.mean(x * x, axis=-1, keepdims=True) + EPS)
    first = x * inverse
    grad = dx_ref[...]
    gattn = jnp.sum(grad * first, axis=0, keepdims=True)
    for f in range(groups):
        gsend[f, :, :slot] = gattn[:, f * slot : (f + 1) * slot]
        gsend[f, :, slot : 2 * slot] = gffn_ref[:, f * slot : (f + 1) * slot]
        gsend[f, :, 2 * slot : 2 * slot + HD] = small_ref[0:1, :]
        gsend[f, :, 2 * slot + HD :] = small_ref[1:2, :]

    def to_slot(f, sender):
        return pltpu.make_async_remote_copy(
            src_ref=gsend.at[f], dst_ref=grecv.at[sender], send_sem=gs_sem.at[f], recv_sem=gr_sem.at[sender],
            device_id={"fsdp": f}, device_id_type=MESH,
        )

    scaled = grad * gain_ref[...]
    dx_ref[...] = gmid_ref[...] + inverse * (scaled - first * jnp.mean(scaled * first, axis=-1, keepdims=True))
    for f in range(groups):
        @pl.when(mine != f)
        def _():
            to_slot(f, mine).start()
    grecv[mine] = gsend[mine]
    for f in range(groups):
        @pl.when(mine != f)
        def _():
            to_slot(f, f).wait_recv()
    tsend[...] = jnp.sum(grecv[...], axis=0)

    def to_part(p, sender):
        return pltpu.make_async_remote_copy(
            src_ref=tsend, dst_ref=trecv.at[sender], send_sem=ts_sem.at[p], recv_sem=tr_sem.at[sender],
            device_id={"tp": p}, device_id_type=MESH,
        )

    for p in range(n):
        @pl.when(me != p)
        def _():
            to_part(p, me).start()
    trecv[me] = tsend[...]
    for p in range(n):
        @pl.when(me != p)
        def _():
            to_part(p, p).wait_recv()
    total_ref[...] = jnp.sum(trecv[...], axis=0)
    for f in range(groups):
        @pl.when(mine != f)
        def _():
            to_slot(f, mine).wait_send()
    for p in range(n):
        @pl.when(me != p)
        def _():
            to_part(p, me).wait_send()
    for t in range(n - 1):
        for s in range(halves):
            for di, d, dist in ways:
                @pl.when(t >= dist)
                def _():
                    item(di, d, t - dist, s, me, False).wait_send()


def final(p, x, gmid, gain, gffn, small, n, groups, cid):
    rows_own, width = gmid.shape
    wide = 2 * (width // groups) + 2 * HD
    vmem = pl.BlockSpec(memory_space=pltpu.VMEM)
    dma = pltpu.SemaphoreType.DMA
    return pl.pallas_call(
        functools.partial(final_kernel, n, groups),
        out_shape=(
            jax.ShapeDtypeStruct((rows_own, width), jnp.float32),
            jax.ShapeDtypeStruct((1, wide), jnp.float32),
        ),
        in_specs=[vmem] * 6,
        out_specs=(vmem, vmem),
        scratch_shapes=[
            pltpu.VMEM((2, n - 1, rows_own, width), jnp.bfloat16),
            pltpu.VMEM((groups, 1, wide), jnp.float32),
            pltpu.VMEM((groups, 1, wide), jnp.float32),
            pltpu.VMEM((1, wide), jnp.float32),
            pltpu.VMEM((n, 1, wide), jnp.float32),
            dma((2, n - 1, 2)), dma((2, n - 1, 2)), dma((groups,)), dma((groups,)), dma((n,)), dma((n,)),
        ],
        compiler_params=pltpu.CompilerParams(
            collective_id=cid, has_side_effects=True, vmem_limit_bytes=40 << 20
        ),
        cost_estimate=pl.CostEstimate(flops=1 << 34, bytes_accessed=200 << 20, transcendentals=0),
        name="final",
    )(p, x, gmid, gain, gffn, small)


def per_device(
    hidden_in,
    grad_out,
    prefix_len,
    positions,
    g_attn,
    w_query,
    w_key,
    w_value,
    w_out,
    q_gain,
    k_gain,
    g_ffn,
    w_gate,
    w_up,
    w_down,
):
    parts = lax.axis_size("tp")
    groups = lax.axis_size("fsdp")
    qc, kc, fc = w_query.shape[1], w_key.shape[1], w_gate.shape[1]
    slot = g_attn.shape[0]
    head_slot = q_gain.shape[0]
    attn_set = lax.all_gather(
        jnp.concatenate([w_query, w_key, w_value, w_out.T], axis=1), "fsdp", axis=0, tiled=True
    )
    ffn_set = lax.all_gather(
        jnp.concatenate([w_gate, w_up, w_down.T], axis=1), "fsdp", axis=0, tiled=True
    )

    def lane_pad(value):
        return jnp.pad(value.astype(jnp.float32), (0, HD - head_slot))

    packed = jnp.concatenate(
        [g_attn.astype(jnp.float32), g_ffn.astype(jnp.float32), lane_pad(q_gain), lane_pad(k_gain)]
    )[None]
    heads, kv_heads = qc // HD, kc // HD
    cos_all, sin_all = rope_tables(positions)
    normed, gain_first, gain_second, gain_rows = entry(hidden_in, packed, parts, groups, head_slot, cid=1)
    middle, grad_all, qkv_low, raw, mixed_low, log_rows = attn(
        hidden_in, grad_out, normed, cos_all, sin_all, gain_rows, prefix_len, attn_set,
        parts, heads, kv_heads, cid=2,
    )
    grad_middle, grad_second, ffn_part, grad_w_ffn = ffn(
        middle, gain_second, grad_all, ffn_set, parts, cid=3
    )

    def spread(value):
        return lax.psum_scatter(value, "fsdp", scatter_dimension=0, tiled=True)

    ffn_own = spread(grad_w_ffn)
    out, grad_normed, grad_small, grad_w_attn = attn_back(
        grad_middle, middle, cos_all, sin_all, log_rows, gain_rows, prefix_len, attn_set,
        normed, qkv_low, raw, mixed_low, ffn_part, parts, heads, kv_heads, cid=4,
    )
    grad_w_attn, ffn_own = lax.optimization_barrier((grad_w_attn, ffn_own))
    attn_own = spread(grad_w_attn).astype(jnp.float32)
    ffn_own = ffn_own.astype(jnp.float32)
    grad_in, sums = final(
        grad_normed, hidden_in, grad_middle, gain_first, grad_second, grad_small, parts, groups, cid=5
    )
    place = lax.axis_index("fsdp") * head_slot
    return (
        out,
        grad_in,
        sums[0, :slot],
        attn_own[:, :qc],
        attn_own[:, qc : qc + kc],
        attn_own[:, qc + kc : qc + 2 * kc],
        attn_own[:, qc + 2 * kc :].T,
        lax.dynamic_slice_in_dim(sums[0, 2 * slot : 2 * slot + HD], place, head_slot),
        lax.dynamic_slice_in_dim(sums[0, 2 * slot + HD :], place, head_slot),
        sums[0, slot : 2 * slot],
        ffn_own[:, :fc],
        ffn_own[:, fc : 2 * fc],
        ffn_own[:, 2 * fc :].T,
    )


def solution(mesh):
    in_specs = (
        P(("fsdp", "tp"), None),
        P(("fsdp", "tp"), None),
        P("fsdp"),
        P("fsdp"),
        P("fsdp"),
        P("fsdp", "tp"),
        P("fsdp", "tp"),
        P("fsdp", "tp"),
        P("tp", "fsdp"),
        P("fsdp"),
        P("fsdp"),
        P("fsdp"),
        P("fsdp", "tp"),
        P("fsdp", "tp"),
        P("tp", "fsdp"),
    )
    out_specs = (
        P(("fsdp", "tp"), None),
        P(("fsdp", "tp"), None),
        P("fsdp"),
        P("fsdp", "tp"),
        P("fsdp", "tp"),
        P("fsdp", "tp"),
        P("tp", "fsdp"),
        P("fsdp"),
        P("fsdp"),
        P("fsdp"),
        P("fsdp", "tp"),
        P("fsdp", "tp"),
        P("tp", "fsdp"),
    )
    return jax.shard_map(
        per_device, mesh=mesh, in_specs=in_specs, out_specs=out_specs, check_vma=False
    )
```

```python
import functools
import math

import jax
import jax.numpy as jnp
from jax import lax
from jax.experimental import pallas as pl
from jax.experimental.pallas import tpu as pltpu
from jax.sharding import PartitionSpec as P

MESH = pl.DeviceIdType.MESH
VMEM_LIMIT = 67043328

HD = 128


EPS = 1e-06
ROPE_BASE = 1000000.0


def rope_tables(places):
    half = HD // 2
    ladder = jnp.arange(half, dtype=jnp.float32) * (2.0 / HD)
    frequency = jnp.exp(-ladder * math.log(ROPE_BASE))
    angle = places.astype(jnp.float32)[:, None] * frequency[None, :]
    cosine, sine = jnp.cos(angle), jnp.sin(angle)
    return jnp.concatenate([cosine, cosine], axis=1), jnp.concatenate([-sine, sine], axis=1)


def greet(me, n, axis):
    barrier = pltpu.get_barrier_semaphore()
    for d in (1, -1):
        @pl.when((me + d >= 0) & (me + d < n))
        def _():
            pl.semaphore_signal(barrier, inc=1, device_id={axis: me + d}, device_id_type=MESH)
    edge = (me == 0) | (me == n - 1)

    @pl.when(edge)
    def _():
        pl.semaphore_wait(barrier, 1)

    @pl.when(~edge)
    def _():
        pl.semaphore_wait(barrier, 2)

def inside(v, n):
    return (v >= 0) & (v < n)

def exchange_plan(n, me):
    return ((0, 1, me), (1, -1, n - 1 - me))


def dot_t(left, right):
    return lax.dot_general(left, right, (((1,), (1,)), ((), ())), preferred_element_type=jnp.float32)


def entry_kernel(
    n, groups, head_slot, x_ref, pack_ref, normed_ref, gattn_ref, gffn_ref, small_ref,
    tokens, grecv, send_sem, recv_sem, gs_sem, gr_sem,
):
    me = lax.axis_index("tp")
    mine = lax.axis_index("fsdp")
    rows_own, width = x_ref.shape
    slot = width // groups
    barrier = pltpu.get_barrier_semaphore()
    for f in range(groups):
        @pl.when(mine != f)
        def _():
            pl.semaphore_signal(barrier, inc=1, device_id={"fsdp": f}, device_id_type=MESH)
    for d in (1, -1):
        @pl.when(inside(me + d, n))
        def _():
            pl.semaphore_signal(barrier, inc=1, device_id={"tp": me + d}, device_id_type=MESH)
    edge = (me == 0) | (me == n - 1)

    @pl.when(edge)
    def _():
        pl.semaphore_wait(barrier, groups)

    @pl.when(~edge)
    def _():
        pl.semaphore_wait(barrier, groups + 1)

    def block(j):
        return pl.ds(pl.multiple_of(j * rows_own, rows_own), rows_own)

    def passing(di, d, k, sender):
        j = sender - d * k
        src = x_ref if k == 0 else tokens.at[block(j)]
        return pltpu.make_async_remote_copy(
            src_ref=src, dst_ref=tokens.at[block(j)], send_sem=send_sem.at[di, k], recv_sem=recv_sem.at[di, k],
            device_id={"tp": sender + d}, device_id_type=MESH,
        )

    def to_peer(f, sender):
        return pltpu.make_async_remote_copy(
            src_ref=pack_ref, dst_ref=grecv.at[sender], send_sem=gs_sem.at[f], recv_sem=gr_sem.at[sender],
            device_id={"fsdp": f}, device_id_type=MESH,
        )

    sides = ((0, 1), (1, -1))
    for di, d in sides:
        @pl.when(inside(me + d, n))
        def _():
            passing(di, d, 0, me).start()
    for f in range(groups):
        @pl.when(mine != f)
        def _():
            to_peer(f, mine).start()
    grecv[mine] = pack_ref[...]
    for f in range(groups):
        @pl.when(mine != f)
        def _():
            to_peer(f, f).wait_recv()
    small_ref[...] = jnp.zeros_like(small_ref)
    for f in range(groups):
        at = slice(f * slot, (f + 1) * slot)
        gattn_ref[:, at] = grecv[f, :, :slot]
        gffn_ref[:, at] = grecv[f, :, slot : 2 * slot]
        for row in range(2):
            part = grecv[f, :, 2 * slot + row * HD : 2 * slot + (row + 1) * HD]
            small_ref[row : row + 1, :] += part if f == 0 else pltpu.roll(part, f * head_slot, 1)

    def normalize(source, at):
        value = source.astype(jnp.float32)
        inverse = lax.rsqrt(jnp.mean(value * value, axis=-1, keepdims=True) + EPS)
        normed_ref[at, :] = (value * inverse * gattn_ref[...]).astype(jnp.bfloat16)

    normalize(x_ref[...], block(me))
    for k in range(1, n):
        for di, d in sides:
            @pl.when(inside(me - d * k, n))
            def _():
                passing(di, d, k - 1, me - d).wait_recv()
            if k < n - 1:
                @pl.when(inside(me - d * k, n) & inside(me + d, n))
                def _():
                    passing(di, d, k, me).start()
        for di, d in sides:
            @pl.when(inside(me - d * k, n))
            def _():
                normalize(tokens[block(me - d * k), :], block(me - d * k))
    for k in range(n - 1):
        for di, d in sides:
            @pl.when(inside(me - d * k, n) & inside(me + d, n))
            def _():
                passing(di, d, k, me).wait_send()
    for f in range(groups):
        @pl.when(mine != f)
        def _():
            to_peer(f, mine).wait_send()


def entry(x, pack, n, groups, head_slot, cid):
    rows_own, width = x.shape
    vmem = pl.BlockSpec(memory_space=pltpu.VMEM)
    dma = pltpu.SemaphoreType.DMA
    return pl.pallas_call(
        functools.partial(entry_kernel, n, groups, head_slot),
        out_shape=(
            jax.ShapeDtypeStruct((rows_own * n, width), jnp.bfloat16),
            jax.ShapeDtypeStruct((1, width), jnp.float32),
            jax.ShapeDtypeStruct((1, width), jnp.float32),
            jax.ShapeDtypeStruct((8, HD), jnp.float32),
        ),
        in_specs=[vmem] * 2,
        out_specs=(vmem,) * 4,
        scratch_shapes=[
            pltpu.VMEM((rows_own * n, width), jnp.bfloat16),
            pltpu.VMEM((groups,) + pack.shape, jnp.float32),
            dma((2, n - 1)), dma((2, n - 1)), dma((groups,)), dma((groups,)),
        ],
        compiler_params=pltpu.CompilerParams(
            collective_id=cid, has_side_effects=True, vmem_limit_bytes=32 << 20
        ),
        cost_estimate=pl.CostEstimate(flops=1 << 34, bytes_accessed=200 << 20, transcendentals=0),
        name="entry",
    )(x, pack)


def attn_kernel(
    n, axis, heads, kv_heads,
    x_ref, go_ref, normed_ref, cos_ref, sin_ref, gain_ref, prefix_ref, w_hbm,
    mid_ref, go_all, qkv, raw, mixed, lse_ref,
    wbuf, part, values_t, rb, load_sem, send_ag, recv_ag, send_rs, recv_rs,
):
    me = lax.axis_index(axis)
    rows_own, width = x_ref.shape
    total = rows_own * n
    qc, kc = heads * HD, kv_heads * HD
    group = heads // kv_heads
    scale = 1.0 / math.sqrt(HD)
    load = pltpu.make_async_copy(w_hbm, wbuf, load_sem.at[0])
    load.start()
    greet(me, n, axis)

    def block(j):
        return pl.ds(pl.multiple_of(j * rows_own, rows_own), rows_own)

    def passing(di, d, k, sender):
        j = sender - d * k
        src = go_ref if k == 0 else go_all.at[block(j)]
        return pltpu.make_async_remote_copy(
            src_ref=src, dst_ref=go_all.at[block(j)], send_sem=send_ag.at[di, k], recv_sem=recv_ag.at[di, k],
            device_id={axis: sender + d}, device_id_type=MESH,
        )

    def owner(d, q):
        return n - 1 - q if d > 0 else q

    def item(di, d, q, sender, first):
        src = part.at[block(owner(d, q))] if first else rb.at[di, q]
        return pltpu.make_async_remote_copy(
            src_ref=src, dst_ref=rb.at[di, q], send_sem=send_rs.at[di, q], recv_sem=recv_rs.at[di, q],
            device_id={axis: sender + d}, device_id_type=MESH,
        )

    sides = ((0, 1), (1, -1))
    ways = exchange_plan(n, me)

    def gather_step(k):
        for di, d in sides:
            if k > 0:
                @pl.when(inside(me - d * k, n))
                def _():
                    passing(di, d, k - 1, me - d).wait_recv()
            if k < n - 1:
                @pl.when(inside(me - d * k, n) & inside(me + d, n))
                def _():
                    passing(di, d, k, me).start()

    def sums_step(t):
        for di, d, dist in ways:
            @pl.when((dist > 0) & (t >= dist))
            def _():
                q = t - dist
                item(di, d, q, me - d, False).wait_recv()
                rb[di, q] = (rb[di, q].astype(jnp.float32) + part[block(owner(d, q)), :].astype(jnp.float32)).astype(rb.dtype)
                item(di, d, q, me, False).start()

    gather_step(0)
    go_all[block(me), :] = go_ref[...]
    lse_ref[...] = jnp.zeros_like(lse_ref)
    load.wait()

    def project(j, carry):
        at = block(j)
        value = jnp.dot(normed_ref[at, :], wbuf[:, : qc + 2 * kc], preferred_element_type=jnp.float32)
        raw[at, :] = value[:, : qc + kc]
        for h in range(heads + kv_heads):
            head = value[:, h * HD : (h + 1) * HD]
            gain = gain_ref[0:1, :] if h < heads else gain_ref[1:2, :]
            scaled = head * lax.rsqrt(jnp.mean(head * head, axis=-1, keepdims=True) + EPS) * gain
            turned = scaled * cos_ref[at, :] + pltpu.roll(scaled, HD // 2, 1) * sin_ref[at, :]
            qkv[at, h * HD : (h + 1) * HD] = turned.astype(jnp.bfloat16)
        qkv[at, qc + kc :] = value[:, qc + kc :].astype(jnp.bfloat16)
        return carry

    lax.fori_loop(0, n, project, 0)
    for g in range(kv_heads):
        values_t[g] = qkv[:, qc + kc + g * HD : qc + kc + (g + 1) * HD].T
    prefix = prefix_ref[0]

    def attend(i, carry):
        @pl.when(i == 2)
        def _():
            gather_step(1)
        j = jnp.where(2 * me < n, n - 1 - i, i)
        at = block(j)
        key_at = lax.broadcasted_iota(jnp.int32, (total, rows_own), 0)
        query_at = lax.broadcasted_iota(jnp.int32, (total, rows_own), 1) + j * rows_own
        seen = (key_at <= query_at) | (key_at < prefix)
        for h in range(heads):
            g = h // group
            ks, hs = qc + g * HD, h * HD
            scores = jnp.where(seen, dot_t(qkv[:, ks : ks + HD], qkv[at, hs : hs + HD]) * scale, -1e30)
            peak = jnp.max(scores, axis=0, keepdims=True)
            raised = jnp.exp(scores - peak)
            weight = jnp.sum(raised, axis=0, keepdims=True)
            lse_ref[h : h + 1, at] = peak + jnp.log(weight)
            shares = (raised * (1.0 / weight)).astype(jnp.bfloat16)
            mixed[at, hs : hs + HD] = jnp.dot(values_t[g], shares, preferred_element_type=jnp.float32).T.astype(jnp.bfloat16)
        cut = width // 4
        for f in range(4):
            cols = pl.ds(f * cut, cut)
            part[at, cols] = dot_t(mixed[at, :], wbuf[cols, qc + 2 * kc :]).astype(jnp.bfloat16)
        for di, d, dist in ways:
            @pl.when((dist == 0) & (i < n - 1))
            def _():
                item(di, d, i, me, True).start()
        return carry

    lax.fori_loop(0, n, attend, 0)
    for t in range(1, n):
        if t < n - 1:
            sums_step(t)
        if t + 1 < n:
            gather_step(t + 1)
    for di, d, dist in ways:
        @pl.when(dist > 0)
        def _():
            item(di, d, n - 1 - dist, me - d, False).wait_recv()
    own = x_ref[...].astype(jnp.float32) + part[block(me), :].astype(jnp.float32)
    @pl.when(me == 0)
    def _():
        mid_ref[...] = own + rb[1, 0].astype(jnp.float32)
    @pl.when(me == n - 1)
    def _():
        mid_ref[...] = own + rb[0, 0].astype(jnp.float32)
    @pl.when((me > 0) & (me < n - 1))
    def _():
        mid_ref[...] = own + rb[0, n - 1 - me].astype(jnp.float32) + rb[1, me].astype(jnp.float32)
    for k in range(n - 1):
        for di, d in sides:
            @pl.when(inside(me - d * k, n) & inside(me + d, n))
            def _():
                passing(di, d, k, me).wait_send()
    for t in range(n - 1):
        for di, d, dist in ways:
            @pl.when(t >= dist)
            def _():
                item(di, d, t - dist, me, False).wait_send()


def attn(x, go, normed, cos2, sin2, gains, prefix, w, n, heads, kv_heads, cid, axis="tp"):
    rows_own, width = x.shape
    total = rows_own * n
    vmem = pl.BlockSpec(memory_space=pltpu.VMEM)
    any_space = pl.BlockSpec(memory_space=pl.ANY)
    dma = pltpu.SemaphoreType.DMA
    cols = (heads + 2 * kv_heads) * HD
    return pl.pallas_call(
        functools.partial(attn_kernel, n, axis, heads, kv_heads),
        out_shape=(
            jax.ShapeDtypeStruct((rows_own, width), jnp.float32),
            jax.ShapeDtypeStruct((total, width), jnp.bfloat16),
            jax.ShapeDtypeStruct((total, cols), jnp.bfloat16),
            jax.ShapeDtypeStruct((total, cols - kv_heads * HD), jnp.float32),
            jax.ShapeDtypeStruct((total, heads * HD), jnp.bfloat16),
            jax.ShapeDtypeStruct((8, total), jnp.float32),
        ),
        in_specs=[vmem] * 6 + [pl.BlockSpec(memory_space=pltpu.SMEM), any_space],
        out_specs=(vmem,) * 6,
        scratch_shapes=[
            pltpu.VMEM(w.shape, jnp.bfloat16),
            pltpu.VMEM((total, width), jnp.bfloat16),
            pltpu.VMEM((kv_heads, HD, total), jnp.bfloat16),
            pltpu.VMEM((2, n - 1, rows_own, width), jnp.bfloat16),
            dma((1,)), dma((2, n - 1)), dma((2, n - 1)), dma((2, n - 1)), dma((2, n - 1)),
        ],
        compiler_params=pltpu.CompilerParams(
            collective_id=cid, has_side_effects=True, vmem_limit_bytes=VMEM_LIMIT
        ),
        cost_estimate=pl.CostEstimate(flops=1 << 34, bytes_accessed=300 << 20, transcendentals=0),
        name="attn",
    )(x, go, normed, cos2, sin2, gains, prefix, w)


def ffn_kernel(
    n, axis, mid_ref, gain_ref, go_ref, w_ref, gmid_ref, gffn_ref, part_ref, gw_ref,
    branch, wbuf, act, gpart, rb, w_sem, out_sem, send_ag, recv_ag, send_rs, recv_rs,
):
    me = lax.axis_index(axis)
    rows_own, width = mid_ref.shape
    hidden = wbuf.shape[2]
    cut = hidden // 3
    wcut = width // 4
    loads = [
        pltpu.make_async_copy(w_ref.at[:, pl.ds(m * hidden, hidden)], wbuf.at[m], w_sem.at[m])
        for m in range(3)
    ]
    for load in loads:
        load.start()

    def block(j):
        return pl.ds(pl.multiple_of(j * rows_own, rows_own), rows_own)

    mid = mid_ref[...]
    inverse = lax.rsqrt(jnp.mean(mid * mid, axis=-1, keepdims=True) + EPS)
    branch[block(me), :] = (mid * inverse * gain_ref[...]).astype(jnp.bfloat16)
    greet(me, n, axis)

    def passing(di, d, k, sender):
        j = sender - d * k
        return pltpu.make_async_remote_copy(
            src_ref=branch.at[block(j)], dst_ref=branch.at[block(j)],
            send_sem=send_ag.at[di, k], recv_sem=recv_ag.at[di, k],
            device_id={axis: sender + d}, device_id_type=MESH,
        )

    sides = ((0, 1), (1, -1))
    for di, d in sides:
        @pl.when(inside(me + d, n))
        def _():
            passing(di, d, 0, me).start()
    for load in loads:
        load.wait()

    def chunk(j):
        at = block(j)
        for f in range(3):
            cols = pl.ds(f * cut, cut)
            gate = jnp.dot(branch[at, :], wbuf[0, :, cols], preferred_element_type=jnp.float32)
            upward = jnp.dot(branch[at, :], wbuf[1, :, cols], preferred_element_type=jnp.float32)
            sig = jax.nn.sigmoid(gate)
            silu = gate * sig
            act[2, at, cols] = (silu * upward).astype(jnp.bfloat16)
            gprod = jnp.dot(go_ref[at, :], wbuf[2, :, cols], preferred_element_type=jnp.float32)
            act[0, at, cols] = (gprod * upward * (sig * (1.0 + gate * (1.0 - sig)))).astype(jnp.bfloat16)
            act[1, at, cols] = (gprod * silu).astype(jnp.bfloat16)
        for f in range(4):
            cols = pl.ds(f * wcut, wcut)
            part_ref[at, cols] = dot_t(act[2, at, :], wbuf[2, cols, :]).astype(jnp.bfloat16)
            gpart[at, cols] = (
                dot_t(act[0, at, :], wbuf[0, cols, :]) + dot_t(act[1, at, :], wbuf[1, cols, :])
            ).astype(jnp.bfloat16)

    def distance(k, carry):
        for di, d in sides:
            @pl.when((k > 0) & inside(me - d * k, n))
            def _():
                passing(di, d, k - 1, me - d).wait_recv()
                @pl.when(inside(me + d, n))
                def _():
                    passing(di, d, k, me).start()
        low = inside(me - k, n)
        high = (k > 0) & inside(me + k, n)
        number = low.astype(jnp.int32) + high.astype(jnp.int32)

        def one(i, c):
            j = jnp.where((i == 0) & low, me - k, me + k)
            chunk(j)
            return c

        lax.fori_loop(0, number, one, 0)
        return carry

    lax.fori_loop(0, n, distance, 0)

    def owner(d, q):
        return n - 1 - q if d > 0 else q

    def item(di, d, q, sender, first):
        src = gpart.at[block(owner(d, q))] if first else rb.at[di, q]
        return pltpu.make_async_remote_copy(
            src_ref=src, dst_ref=rb.at[di, q], send_sem=send_rs.at[di, q], recv_sem=recv_rs.at[di, q],
            device_id={axis: sender + d}, device_id_type=MESH,
        )

    ways = ((0, 1, me), (1, -1, n - 1 - me))
    for q in range(n - 1):
        for di, d, dist in ways:
            @pl.when(dist == 0)
            def _():
                item(di, d, q, me, True).start()

    tile = width // 4

    def leave(m, r):
        return pltpu.make_async_copy(
            wbuf.at[m, pl.ds(pl.multiple_of(r * tile, tile), tile)],
            gw_ref.at[pl.ds(pl.multiple_of(r * tile, tile), tile), pl.ds(m * hidden, hidden)],
            out_sem.at[m, r],
        )

    def weights(m, left):
        def one(r, c):
            at = pl.ds(pl.multiple_of(r * tile, tile), tile)
            wbuf[m, at, :] = lax.dot_general(
                left[:, at], act[m], (((0,), (0,)), ((), ())), preferred_element_type=jnp.float32
            ).astype(jnp.bfloat16)
            leave(m, r).start()
            return c

        lax.fori_loop(0, 4, one, 0)

    todo = [(2, go_ref), (0, branch), (1, branch)]
    for t in range(1, n):
        if todo:
            weights(*todo.pop(0))
        if t == n - 1:
            while todo:
                weights(*todo.pop(0))
            break
        for di, d, dist in ways:
            @pl.when((dist > 0) & (t >= dist))
            def _():
                q = t - dist
                item(di, d, q, me - d, False).wait_recv()
                rb[di, q] = (rb[di, q].astype(jnp.float32) + gpart[block(owner(d, q)), :].astype(jnp.float32)).astype(rb.dtype)
                item(di, d, q, me, False).start()
    for di, d, dist in ways:
        @pl.when(dist > 0)
        def _():
            item(di, d, n - 1 - dist, me - d, False).wait_recv()
    @pl.when(me == 0)
    def _():
        gmid_ref[...] = gpart[block(0), :].astype(jnp.float32) + rb[1, 0].astype(jnp.float32)
    @pl.when(me == n - 1)
    def _():
        gmid_ref[...] = gpart[block(n - 1), :].astype(jnp.float32) + rb[0, 0].astype(jnp.float32)
    @pl.when((me > 0) & (me < n - 1))
    def _():
        gmid_ref[...] = gpart[block(me), :].astype(jnp.float32) + rb[0, n - 1 - me].astype(jnp.float32) + rb[1, me].astype(jnp.float32)
    mid = mid_ref[...]
    inverse = lax.rsqrt(jnp.mean(mid * mid, axis=-1, keepdims=True) + EPS)
    unit = mid * inverse
    grad = gmid_ref[...]
    gffn_ref[...] = jnp.sum(grad * unit, axis=0, keepdims=True)
    scaled = grad * gain_ref[...]
    gmid_ref[...] = go_ref[block(me), :].astype(jnp.float32) + inverse * (scaled - unit * jnp.mean(scaled * unit, axis=-1, keepdims=True))

    for k in range(n - 1):
        for di, d in sides:
            @pl.when(inside(me - d * k, n) & inside(me + d, n))
            def _():
                passing(di, d, k, me).wait_send()
    for t in range(n - 1):
        for di, d, dist in ways:
            @pl.when(t >= dist)
            def _():
                item(di, d, t - dist, me, False).wait_send()
    for m in range(3):
        for r in range(4):
            leave(m, r).wait()


def ffn(mid, gain, go, w, n, cid, axis="tp"):
    rows_own, width = mid.shape
    total = rows_own * n
    hidden = w.shape[1] // 3
    vmem = pl.BlockSpec(memory_space=pltpu.VMEM)
    any_space = pl.BlockSpec(memory_space=pl.ANY)
    dma = pltpu.SemaphoreType.DMA
    return pl.pallas_call(
        functools.partial(ffn_kernel, n, axis),
        out_shape=(
            jax.ShapeDtypeStruct((rows_own, width), jnp.float32),
            jax.ShapeDtypeStruct((1, width), jnp.float32),
            jax.ShapeDtypeStruct((total, width), jnp.bfloat16),
            jax.ShapeDtypeStruct(w.shape, jnp.bfloat16),
        ),
        in_specs=[vmem, vmem, vmem, any_space],
        out_specs=(vmem, vmem, vmem, any_space),
        scratch_shapes=[
            pltpu.VMEM((total, width), jnp.bfloat16),
            pltpu.VMEM((3, width, hidden), jnp.bfloat16),
            pltpu.VMEM((3, total, hidden), jnp.bfloat16),
            pltpu.VMEM((total, width), jnp.bfloat16),
            pltpu.VMEM((2, n - 1, rows_own, width), jnp.bfloat16),
            dma((3,)), dma((3, 4)), dma((2, n - 1)), dma((2, n - 1)), dma((2, n - 1)), dma((2, n - 1)),
        ],
        compiler_params=pltpu.CompilerParams(
            collective_id=cid, has_side_effects=True, vmem_limit_bytes=VMEM_LIMIT
        ),
        cost_estimate=pl.CostEstimate(
            flops=18 * total * width * hidden, bytes_accessed=12 * width * hidden, transcendentals=0
        ),
        name="ffn",
    )(mid, gain, go, w)


def unroll_rot(value, cos2, sin2):
    return value * cos2 - pltpu.roll(value, HD // 2, 1) * sin2


def attn_back_kernel(
    n, axis, heads, kv_heads,
    gmid_ref, mid_ref, cos_ref, sin_ref, lse_ref, gain_ref, prefix_ref,
    w_hbm, normed_hbm, qkv_hbm, raw_hbm, mixed_hbm, part_hbm,
    out_ref, gn_ref, gsum_ref, gw_ref,
    wbuf, normed, qkv, raw, mixed, part, gm, gmix, keys_t, dk, dv, gqkv, rb,
    load_sem, out_sem, send_ag, recv_ag, send_rs, recv_rs,
):
    me = lax.axis_index(axis)
    rows_own, width = gmid_ref.shape
    total = rows_own * n
    qc, kc = heads * HD, kv_heads * HD
    group = heads // kv_heads
    scale = 1.0 / math.sqrt(HD)
    pairs = ((w_hbm, wbuf), (qkv_hbm, qkv), (raw_hbm, raw), (part_hbm, part), (normed_hbm, normed), (mixed_hbm, mixed))
    loads = [pltpu.make_async_copy(src, dst, load_sem.at[i]) for i, (src, dst) in enumerate(pairs)]
    for load in loads:
        load.start()

    def block(j):
        return pl.ds(pl.multiple_of(j * rows_own, rows_own), rows_own)

    gm[block(me), :] = gmid_ref[...].astype(jnp.bfloat16)
    dk[...] = jnp.zeros_like(dk)
    dv[...] = jnp.zeros_like(dv)
    gsum_ref[...] = jnp.zeros_like(gsum_ref)
    greet(me, n, axis)

    def passing(di, d, k, sender):
        j = sender - d * k
        return pltpu.make_async_remote_copy(
            src_ref=gm.at[block(j)], dst_ref=gm.at[block(j)],
            send_sem=send_ag.at[di, k], recv_sem=recv_ag.at[di, k],
            device_id={axis: sender + d}, device_id_type=MESH,
        )

    def owner(d, q):
        return n - 1 - q if d > 0 else q

    def item(di, d, q, sender, first):
        src = part.at[block(owner(d, q))] if first else rb.at[di, q]
        return pltpu.make_async_remote_copy(
            src_ref=src, dst_ref=rb.at[di, q], send_sem=send_rs.at[di, q], recv_sem=recv_rs.at[di, q],
            device_id={axis: sender + d}, device_id_type=MESH,
        )

    sides = ((0, 1), (1, -1))
    ways = exchange_plan(n, me)
    for di, d in sides:
        @pl.when(inside(me + d, n))
        def _():
            passing(di, d, 0, me).start()
    for load in loads[:3]:
        load.wait()
    for g in range(kv_heads):
        keys_t[g] = qkv[:, qc + g * HD : qc + (g + 1) * HD].T
    loads[3].wait()
    prefix = prefix_ref[0]

    def unit_of(at, first):
        value = raw[at, first : first + HD]
        inverse = lax.rsqrt(jnp.mean(value * value, axis=-1, keepdims=True) + EPS)
        return value * inverse, inverse

    def normed_back(grad, at, first, gain, place):
        unit, inverse = unit_of(at, first)
        turned = unroll_rot(grad, cos_ref[at, :], sin_ref[at, :])
        gsum_ref[place : place + 1, :] += jnp.sum(turned * unit, axis=0, keepdims=True)
        scaled = turned * gain
        return (inverse * (scaled - unit * jnp.mean(scaled * unit, axis=-1, keepdims=True))).astype(jnp.bfloat16)

    def chunk(j):
        at = block(j)
        gmix[...] = jnp.dot(gm[at, :], wbuf[:, qc + 2 * kc :], preferred_element_type=jnp.float32).astype(jnp.bfloat16)
        key_at = lax.broadcasted_iota(jnp.int32, (total, rows_own), 0)
        query_at = lax.broadcasted_iota(jnp.int32, (total, rows_own), 1) + j * rows_own
        seen = (key_at <= query_at) | (key_at < prefix)
        for h in range(heads):
            g = h // group
            ks, vs, hs = qc + g * HD, qc + kc + g * HD, h * HD
            q = qkv[at, hs : hs + HD]
            gx = gmix[:, hs : hs + HD]
            scores = dot_t(qkv[:, ks : ks + HD], q) * scale
            shares = jnp.where(seen, jnp.exp(scores - lse_ref[h : h + 1, at]), 0.0)
            grad_shares = dot_t(qkv[:, vs : vs + HD], gx)
            delta = jnp.sum(grad_shares * shares, axis=0, keepdims=True)
            low = (shares * (grad_shares - delta) * scale).astype(jnp.bfloat16)
            gcols = pl.ds(g * HD, HD)
            dk[:, gcols] += jnp.dot(low, q, preferred_element_type=jnp.float32)
            dv[:, gcols] += jnp.dot(shares.astype(jnp.bfloat16), gx, preferred_element_type=jnp.float32)
            dq = jnp.dot(keys_t[g], low, preferred_element_type=jnp.float32).T
            gqkv[at, hs : hs + HD] = normed_back(dq, at, hs, gain_ref[0:1, :], 0)

    def sums_step(t):
        for di, d, dist in ways:
            @pl.when((dist > 0) & (t >= dist))
            def _():
                q = t - dist
                item(di, d, q, me - d, False).wait_recv()
                rb[di, q] = (rb[di, q].astype(jnp.float32) + part[block(owner(d, q)), :].astype(jnp.float32)).astype(rb.dtype)
                item(di, d, q, me, False).start()

    def distance(k, carry):
        for di, d in sides:
            @pl.when((k > 0) & inside(me - d * k, n))
            def _():
                passing(di, d, k - 1, me - d).wait_recv()
                @pl.when(inside(me + d, n))
                def _():
                    passing(di, d, k, me).start()

        for di, d, dist in ways:
            @pl.when((k == 1) & (dist == 0))
            def _():
                for q in range(n - 1):
                    item(di, d, q, me, True).start()

        @pl.when(k > 1)
        def _():
            sums_step(k - 1)

        low = inside(me - k, n)
        high = (k > 0) & inside(me + k, n)
        number = low.astype(jnp.int32) + high.astype(jnp.int32)

        def one(i, c):
            chunk(jnp.where((i == 0) & low, me - k, me + k))
            return c

        lax.fori_loop(0, number, one, 0)
        return carry

    lax.fori_loop(0, n, distance, 0)

    for load in loads[4:]:
        load.wait()

    def finish(j, carry):
        at = block(j)
        for g in range(kv_heads):
            ks, vs = qc + g * HD, qc + kc + g * HD
            gqkv[at, ks : ks + HD] = normed_back(dk[at, g * HD : (g + 1) * HD], at, ks, gain_ref[1:2, :], 1)
            gqkv[at, vs : vs + HD] = dv[at, g * HD : (g + 1) * HD].astype(jnp.bfloat16)
        cut = width // 4
        for f in range(4):
            cols = pl.ds(f * cut, cut)
            gn_ref[at, cols] = dot_t(gqkv[at, :], wbuf[cols, : qc + 2 * kc]).astype(jnp.bfloat16)
        return carry

    lax.fori_loop(0, n, finish, 0)

    tile = width // 4

    def leave(r):
        at = pl.ds(pl.multiple_of(r * tile, tile), tile)
        return pltpu.make_async_copy(wbuf.at[at], gw_ref.at[at], out_sem.at[r])

    def weights(r, carry):
        at = pl.ds(pl.multiple_of(r * tile, tile), tile)
        wbuf[at, : qc + 2 * kc] = lax.dot_general(
            normed[:, at], gqkv[...], (((0,), (0,)), ((), ())), preferred_element_type=jnp.float32
        ).astype(jnp.bfloat16)
        wbuf[at, qc + 2 * kc :] = lax.dot_general(
            gm[:, at], mixed[...], (((0,), (0,)), ((), ())), preferred_element_type=jnp.float32
        ).astype(jnp.bfloat16)
        leave(r).start()
        return carry

    lax.fori_loop(0, 4, weights, 0)

    for di, d, dist in ways:
        @pl.when(dist > 0)
        def _():
            item(di, d, n - 1 - dist, me - d, False).wait_recv()
    own = mid_ref[...] + part[block(me), :].astype(jnp.float32)
    @pl.when(me == 0)
    def _():
        out_ref[...] = (own + rb[1, 0].astype(jnp.float32)).astype(out_ref.dtype)
    @pl.when(me == n - 1)
    def _():
        out_ref[...] = (own + rb[0, 0].astype(jnp.float32)).astype(out_ref.dtype)
    @pl.when((me > 0) & (me < n - 1))
    def _():
        out_ref[...] = (own + rb[0, n - 1 - me].astype(jnp.float32) + rb[1, me].astype(jnp.float32)).astype(out_ref.dtype)

    for k in range(n - 1):
        for di, d in sides:
            @pl.when(inside(me - d * k, n) & inside(me + d, n))
            def _():
                passing(di, d, k, me).wait_send()
    for t in range(n - 1):
        for di, d, dist in ways:
            @pl.when(t >= dist)
            def _():
                item(di, d, t - dist, me, False).wait_send()
    for r in range(4):
        leave(r).wait()


def attn_back(gmid, mid, cos2, sin2, lse, gains, prefix, w, normed, qkv, raw, mixed, part, n, heads, kv_heads, cid, axis="tp"):
    rows_own, width = gmid.shape
    total = rows_own * n
    vmem = pl.BlockSpec(memory_space=pltpu.VMEM)
    any_space = pl.BlockSpec(memory_space=pl.ANY)
    dma = pltpu.SemaphoreType.DMA
    return pl.pallas_call(
        functools.partial(attn_back_kernel, n, axis, heads, kv_heads),
        out_shape=(
            jax.ShapeDtypeStruct((rows_own, width), jnp.bfloat16),
            jax.ShapeDtypeStruct((total, width), jnp.bfloat16),
            jax.ShapeDtypeStruct((8, HD), jnp.float32),
            jax.ShapeDtypeStruct(w.shape, jnp.bfloat16),
        ),
        in_specs=[vmem] * 6 + [pl.BlockSpec(memory_space=pltpu.SMEM)] + [any_space] * 6,
        out_specs=(vmem, vmem, vmem, any_space),
        scratch_shapes=[
            pltpu.VMEM(w.shape, jnp.bfloat16),
            pltpu.VMEM(normed.shape, jnp.bfloat16),
            pltpu.VMEM(qkv.shape, jnp.bfloat16),
            pltpu.VMEM(raw.shape, jnp.float32),
            pltpu.VMEM(mixed.shape, jnp.bfloat16),
            pltpu.VMEM(part.shape, jnp.bfloat16),
            pltpu.VMEM((total, width), jnp.bfloat16),
            pltpu.VMEM((rows_own, heads * HD), jnp.bfloat16),
            pltpu.VMEM((kv_heads, HD, total), jnp.bfloat16),
            pltpu.VMEM((total, kv_heads * HD), jnp.float32),
            pltpu.VMEM((total, kv_heads * HD), jnp.float32),
            pltpu.VMEM(qkv.shape, jnp.bfloat16),
            pltpu.VMEM((2, n - 1, rows_own, width), jnp.bfloat16),
            dma((6,)), dma((4,)), dma((2, n - 1)), dma((2, n - 1)), dma((2, n - 1)), dma((2, n - 1)),
        ],
        compiler_params=pltpu.CompilerParams(
            collective_id=cid, has_side_effects=True, vmem_limit_bytes=VMEM_LIMIT
        ),
        cost_estimate=pl.CostEstimate(flops=30 * total * width * HD, bytes_accessed=40 * total * width, transcendentals=0),
        name="attn_back",
    )(gmid, mid, cos2, sin2, lse, gains, prefix, w, normed, qkv, raw, mixed, part)


def final_kernel(
    n, groups, p_ref, x_ref, gmid_ref, gain_ref, gffn_ref, small_ref, dx_ref, total_ref,
    rb, gsend, grecv, tsend, trecv, send_sem, recv_sem, gs_sem, gr_sem, ts_sem, tr_sem,
):
    me = lax.axis_index("tp")
    mine = lax.axis_index("fsdp")
    rows_own, width = dx_ref.shape
    slot = width // groups
    barrier = pltpu.get_barrier_semaphore()
    for f in range(groups):
        @pl.when(mine != f)
        def _():
            pl.semaphore_signal(barrier, inc=1, device_id={"fsdp": f}, device_id_type=MESH)
    for p in range(n):
        @pl.when(me != p)
        def _():
            pl.semaphore_signal(barrier, inc=1, device_id={"tp": p}, device_id_type=MESH)
    pl.semaphore_wait(barrier, groups + n - 2)

    def block(j):
        return pl.ds(pl.multiple_of(j * rows_own, rows_own), rows_own)

    def owner(d, q):
        return n - 1 - q if d > 0 else q

    halves = 2
    half = rows_own // halves

    def item(di, d, q, s, sender, first):
        at = pl.ds(s * half, half)
        src = p_ref.at[pl.ds(pl.multiple_of(owner(d, q) * rows_own + s * half, half), half)] if first else rb.at[di, q, at]
        return pltpu.make_async_remote_copy(
            src_ref=src, dst_ref=rb.at[di, q, at], send_sem=send_sem.at[di, q, s], recv_sem=recv_sem.at[di, q, s],
            device_id={"tp": sender + d}, device_id_type=MESH,
        )

    ways = exchange_plan(n, me)
    for q in range(n - 1):
        for s in range(halves):
            for di, d, dist in ways:
                @pl.when(dist == 0)
                def _():
                    item(di, d, q, s, me, True).start()
    for t in range(1, n - 1):
        for s in range(halves):
            for di, d, dist in ways:
                @pl.when((dist > 0) & (t >= dist))
                def _():
                    q = t - dist
                    at = pl.ds(s * half, half)
                    item(di, d, q, s, me - d, False).wait_recv()
                    mine_at = pl.ds(pl.multiple_of(owner(d, q) * rows_own + s * half, half), half)
                    rb[di, q, at, :] = (rb[di, q, at, :].astype(jnp.float32) + p_ref[mine_at, :].astype(jnp.float32)).astype(rb.dtype)
                    item(di, d, q, s, me, False).start()
    for s in range(halves):
        for di, d, dist in ways:
            @pl.when(dist > 0)
            def _():
                item(di, d, n - 1 - dist, s, me - d, False).wait_recv()
    own = p_ref[block(me), :].astype(jnp.float32)
    @pl.when(me == 0)
    def _():
        dx_ref[...] = own + rb[1, 0].astype(jnp.float32)
    @pl.when(me == n - 1)
    def _():
        dx_ref[...] = own + rb[0, 0].astype(jnp.float32)
    @pl.when((me > 0) & (me < n - 1))
    def _():
        dx_ref[...] = own + rb[0, n - 1 - me].astype(jnp.float32) + rb[1, me].astype(jnp.float32)

    x = x_ref[...].astype(jnp.float32)
    inverse = lax.rsqrt(jnp.mean(x * x, axis=-1, keepdims=True) + EPS)
    first = x * inverse
    grad = dx_ref[...]
    gattn = jnp.sum(grad * first, axis=0, keepdims=True)
    for f in range(groups):
        gsend[f, :, :slot] = gattn[:, f * slot : (f + 1) * slot]
        gsend[f, :, slot : 2 * slot] = gffn_ref[:, f * slot : (f + 1) * slot]
        gsend[f, :, 2 * slot : 2 * slot + HD] = small_ref[0:1, :]
        gsend[f, :, 2 * slot + HD :] = small_ref[1:2, :]

    def to_slot(f, sender):
        return pltpu.make_async_remote_copy(
            src_ref=gsend.at[f], dst_ref=grecv.at[sender], send_sem=gs_sem.at[f], recv_sem=gr_sem.at[sender],
            device_id={"fsdp": f}, device_id_type=MESH,
        )

    scaled = grad * gain_ref[...]
    dx_ref[...] = gmid_ref[...] + inverse * (scaled - first * jnp.mean(scaled * first, axis=-1, keepdims=True))
    for f in range(groups):
        @pl.when(mine != f)
        def _():
            to_slot(f, mine).start()
    grecv[mine] = gsend[mine]
    for f in range(groups):
        @pl.when(mine != f)
        def _():
            to_slot(f, f).wait_recv()
    tsend[...] = jnp.sum(grecv[...], axis=0)

    def to_part(p, sender):
        return pltpu.make_async_remote_copy(
            src_ref=tsend, dst_ref=trecv.at[sender], send_sem=ts_sem.at[p], recv_sem=tr_sem.at[sender],
            device_id={"tp": p}, device_id_type=MESH,
        )

    for p in range(n):
        @pl.when(me != p)
        def _():
            to_part(p, me).start()
    trecv[me] = tsend[...]
    for p in range(n):
        @pl.when(me != p)
        def _():
            to_part(p, p).wait_recv()
    total_ref[...] = jnp.sum(trecv[...], axis=0)
    for f in range(groups):
        @pl.when(mine != f)
        def _():
            to_slot(f, mine).wait_send()
    for p in range(n):
        @pl.when(me != p)
        def _():
            to_part(p, me).wait_send()
    for t in range(n - 1):
        for s in range(halves):
            for di, d, dist in ways:
                @pl.when(t >= dist)
                def _():
                    item(di, d, t - dist, s, me, False).wait_send()


def final(p, x, gmid, gain, gffn, small, n, groups, cid):
    rows_own, width = gmid.shape
    wide = 2 * (width // groups) + 2 * HD
    vmem = pl.BlockSpec(memory_space=pltpu.VMEM)
    dma = pltpu.SemaphoreType.DMA
    return pl.pallas_call(
        functools.partial(final_kernel, n, groups),
        out_shape=(
            jax.ShapeDtypeStruct((rows_own, width), jnp.float32),
            jax.ShapeDtypeStruct((1, wide), jnp.float32),
        ),
        in_specs=[vmem] * 6,
        out_specs=(vmem, vmem),
        scratch_shapes=[
            pltpu.VMEM((2, n - 1, rows_own, width), jnp.bfloat16),
            pltpu.VMEM((groups, 1, wide), jnp.float32),
            pltpu.VMEM((groups, 1, wide), jnp.float32),
            pltpu.VMEM((1, wide), jnp.float32),
            pltpu.VMEM((n, 1, wide), jnp.float32),
            dma((2, n - 1, 2)), dma((2, n - 1, 2)), dma((groups,)), dma((groups,)), dma((n,)), dma((n,)),
        ],
        compiler_params=pltpu.CompilerParams(
            collective_id=cid, has_side_effects=True, vmem_limit_bytes=40 << 20
        ),
        cost_estimate=pl.CostEstimate(flops=1 << 34, bytes_accessed=200 << 20, transcendentals=0),
        name="final",
    )(p, x, gmid, gain, gffn, small)


def per_device(
    hidden_in,
    grad_out,
    prefix_len,
    positions,
    g_attn,
    w_query,
    w_key,
    w_value,
    w_out,
    q_gain,
    k_gain,
    g_ffn,
    w_gate,
    w_up,
    w_down,
):
    parts = lax.axis_size("tp")
    groups = lax.axis_size("fsdp")
    qc, kc, fc = w_query.shape[1], w_key.shape[1], w_gate.shape[1]
    slot = g_attn.shape[0]
    head_slot = q_gain.shape[0]
    attn_set = lax.all_gather(
        jnp.concatenate([w_query, w_key, w_value, w_out.T], axis=1), "fsdp", axis=0, tiled=True
    )
    ffn_set = lax.all_gather(
        jnp.concatenate([w_gate, w_up, w_down.T], axis=1), "fsdp", axis=0, tiled=True
    )

    def lane_pad(value):
        return jnp.pad(value.astype(jnp.float32), (0, HD - head_slot))

    packed = jnp.concatenate(
        [g_attn.astype(jnp.float32), g_ffn.astype(jnp.float32), lane_pad(q_gain), lane_pad(k_gain)]
    )[None]
    heads, kv_heads = qc // HD, kc // HD
    cos_all, sin_all = rope_tables(positions)
    normed, gain_first, gain_second, gain_rows = entry(hidden_in, packed, parts, groups, head_slot, cid=1)
    middle, grad_all, qkv_low, raw, mixed_low, log_rows = attn(
        hidden_in, grad_out, normed, cos_all, sin_all, gain_rows, prefix_len, attn_set,
        parts, heads, kv_heads, cid=2,
    )
    grad_middle, grad_second, ffn_part, grad_w_ffn = ffn(
        middle, gain_second, grad_all, ffn_set, parts, cid=3
    )

    def spread(value):
        return lax.psum_scatter(value, "fsdp", scatter_dimension=0, tiled=True)

    ffn_own = spread(grad_w_ffn)
    out, grad_normed, grad_small, grad_w_attn = attn_back(
        grad_middle, middle, cos_all, sin_all, log_rows, gain_rows, prefix_len, attn_set,
        normed, qkv_low, raw, mixed_low, ffn_part, parts, heads, kv_heads, cid=4,
    )
    attn_own = spread(grad_w_attn)
    grad_in, sums = final(
        grad_normed, hidden_in, grad_middle, gain_first, grad_second, grad_small, parts, groups, cid=5
    )
    ffn_own = ffn_own.astype(jnp.float32)
    gate_own, up_own, down_own = ffn_own[:, :fc], ffn_own[:, fc : 2 * fc], ffn_own[:, 2 * fc :].T
    attn_own, gate_own, up_own, down_own = lax.optimization_barrier((attn_own, gate_own, up_own, down_own))
    attn_own = attn_own.astype(jnp.float32)
    place = lax.axis_index("fsdp") * head_slot
    return (
        out,
        grad_in,
        sums[0, :slot],
        attn_own[:, :qc],
        attn_own[:, qc : qc + kc],
        attn_own[:, qc + kc : qc + 2 * kc],
        attn_own[:, qc + 2 * kc :].T,
        lax.dynamic_slice_in_dim(sums[0, 2 * slot : 2 * slot + HD], place, head_slot),
        lax.dynamic_slice_in_dim(sums[0, 2 * slot + HD :], place, head_slot),
        sums[0, slot : 2 * slot],
        gate_own,
        up_own,
        down_own,
    )


def solution(mesh):
    in_specs = (
        P(("fsdp", "tp"), None),
        P(("fsdp", "tp"), None),
        P("fsdp"),
        P("fsdp"),
        P("fsdp"),
        P("fsdp", "tp"),
        P("fsdp", "tp"),
        P("fsdp", "tp"),
        P("tp", "fsdp"),
        P("fsdp"),
        P("fsdp"),
        P("fsdp"),
        P("fsdp", "tp"),
        P("fsdp", "tp"),
        P("tp", "fsdp"),
    )
    out_specs = (
        P(("fsdp", "tp"), None),
        P(("fsdp", "tp"), None),
        P("fsdp"),
        P("fsdp", "tp"),
        P("fsdp", "tp"),
        P("fsdp", "tp"),
        P("tp", "fsdp"),
        P("fsdp"),
        P("fsdp"),
        P("fsdp"),
        P("fsdp", "tp"),
        P("fsdp", "tp"),
        P("tp", "fsdp"),
    )
    return jax.shard_map(
        per_device, mesh=mesh, in_specs=in_specs, out_specs=out_specs, check_vma=False
    )
```
